32 devices in a mesh: row: 2 (over y), col: 16 (over z, x, core).
Axes of the slice: x: 2, y: 2, z: 4, core: 2. Of those that a mesh axis runs over, the one named last changes fastest.
Arguments:
- velocity: bfloat16 [3, 512, 1024, 256], P(None, 'row', 'col'), may hold values from -6 to 6
- adj_temp: bfloat16 [512, 1024, 256], P('row', 'col'), may hold values from -6 to 6
- radial_div: bfloat16 [256, 256], replicated, may hold values from -0.375 to 0.375
- reciprocal_distance: float32 [256], replicated, may hold values from 0.002 to 0.02
- radial_basis: bfloat16 [168, 256, 256], P('row'), may hold values from -0.375 to 0.375
- radial_eig: float32 [168, 256], P('row'), may hold values from 0.5 to 8
- axial_diff: bfloat16 [1024, 1024], replicated, may hold values from -0.1875 to 0.1875
- axial_basis: bfloat16 [1024, 1024], replicated, may hold values from -0.1875 to 0.1875
- axial_eig: float32 [1024], replicated, may hold values from 0.5 to 8
Outputs:
- new_temp: float32 [168, 2, 1024, 256], P('row', None, 'col')
The draws below stay inside these ranges and needn't reach their ends.
All inputs are finite; a program needn't handle non-finite values.
Results may differ from the reference program's by a relative error of at most 0.0055.
Values may be sent and summed in bfloat16 or wider, within the bound.
A program may use at most 256 MiB of HBM per device.

```python
import math
import jax
import jax.numpy as jnp
from jax import lax

NT = 512
NR = 256
NZ = 1024
MODES = 168


def level_of(key, dims, pieces, smallest, largest):
    def one(dim, parts):
        draws = jax.random.uniform(jax.random.fold_in(jax.random.fold_in(key, 6), dim), (parts,), jnp.float32, smallest / len(pieces), largest / len(pieces))
        return jnp.repeat(jnp.exp(draws), dims[dim] // parts).reshape((-1,) + (1,) * (len(dims) - dim - 1))

    loudness = one(*pieces[0])
    for cut in pieces[1:]:
        loudness = loudness * one(*cut)
    return loudness


def scatter_about(own_key, extent, deviation, limit, split=(), held_as=jnp.bfloat16):
    result = jax.random.normal(own_key, extent, jnp.float32) * deviation
    if len(split) > 0:
        result = level_of(own_key, extent, split, -0.22, 0.18) * result
    return jnp.clip(result, min=-limit, max=limit).astype(held_as)


def setup_inputs(seed: int = 0) -> dict:
    arg_keys = jax.random.split(jax.random.key(seed), 10)
    velocity = scatter_about(arg_keys[0], (3, NT, NZ, NR), 1.0, 6.0, ((1, 2), (2, 16)))
    adj_temp = scatter_about(arg_keys[1], (NT, NZ, NR), 1.0, 6.0, ((0, 2), (1, 16)))
    radial_div = scatter_about(arg_keys[2], (NR, NR), NR ** -0.5, 0.375)
    reciprocal_distance = jnp.clip(jnp.exp(jax.random.uniform(arg_keys[3], (NR,), jnp.float32, math.log(0.002), math.log(0.02))), 0.002, 0.02)
    radial_basis = scatter_about(arg_keys[4], (MODES, NR, NR), NR ** -0.5, 0.375, ((0, 2),))
    radial_eig = jnp.clip(jnp.exp(math.log(8.0) - 2.7725887 * jax.random.uniform(arg_keys[5], (MODES, NR), jnp.float32) ** level_of(arg_keys[5], (MODES, NR), ((0, 2),), -0.2, 0.2)), 0.5, 8.0)
    axial_diff = scatter_about(arg_keys[6], (NZ, NZ), NZ ** -0.5, 0.1875)
    axial_basis = scatter_about(arg_keys[7], (NZ, NZ), NZ ** -0.5, 0.1875)
    axial_eig = jnp.clip(jnp.exp(jax.random.uniform(arg_keys[8], (NZ,), jnp.float32, math.log(0.5), math.log(8.0))), 0.5, 8.0)
    return dict(velocity=velocity, adj_temp=adj_temp, radial_div=radial_div, reciprocal_distance=reciprocal_distance, radial_basis=radial_basis, radial_eig=radial_eig, axial_diff=axial_diff, axial_basis=axial_basis, axial_eig=axial_eig)


HEAT_OFFSET = 1.0

def azimuth_table(first_mode, mode_count, first_angle, angle_count, circle):
    mode_ids = jnp.arange(mode_count, dtype=jnp.int32) + first_mode
    angle_ids = jnp.arange(angle_count, dtype=jnp.int32) + first_angle
    phase_index = mode_ids[:, None] * angle_ids[None, :] % circle
    angle_value = phase_index.astype(jnp.float32) * (2.0 * math.pi / circle)
    norm_factor = 1.0 / math.sqrt(circle)
    wave_table = jnp.stack([jnp.cos(angle_value) * norm_factor, -jnp.sin(angle_value) * norm_factor], axis=1)
    return wave_table.astype(jnp.bfloat16).reshape(mode_count * 2, angle_count)

def reference(velocity, adj_temp, radial_div, reciprocal_distance, radial_basis, radial_eig, axial_diff, axial_basis, axial_eig):
    highest = lax.Precision.HIGHEST
    fluxes = (velocity.astype(jnp.float32) * adj_temp.astype(jnp.float32)[None]).astype(jnp.bfloat16)
    fields = jnp.concatenate([fluxes, adj_temp[None]], axis=0)
    wave_table = azimuth_table(0, MODES, 0, NT, NT).astype(jnp.float32)

    def transform(field):
        flat_field = field.reshape(NT, NZ * NR).astype(jnp.float32)
        return jnp.dot(wave_table, flat_field, precision=highest).astype(jnp.bfloat16)
    harmonic_amplitudes = lax.map(transform, fields).reshape(4, MODES, 2, NZ, NR)
    harmonic_amplitudes = jnp.moveaxis(harmonic_amplitudes, 1, 0)
    axial_matrix = axial_diff.astype(jnp.float32)
    axial_vectors = axial_basis.astype(jnp.float32)
    divergence = radial_div.astype(jnp.float32)
    mode_values = jnp.arange(MODES).astype(jnp.float32)

    def one_mode(items):
        harmonic_amplitude, radial_vectors, radial_values, harmonic_coefficient = items
        radial_flux = harmonic_amplitude[0]
        angular_flux = harmonic_amplitude[1]
        axial_flux = harmonic_amplitude[2]
        thermal_state = harmonic_amplitude[3]
        cylinder_aggregate = jnp.einsum('pzj,rj->pzr', radial_flux.astype(jnp.float32), divergence, precision=highest)
        eigenbasis_projection = jnp.stack([-angular_flux[1], angular_flux[0]], axis=0).astype(jnp.float32)
        forcing_contribution = (HEAT_OFFSET * thermal_state.astype(jnp.float32) + cylinder_aggregate + harmonic_coefficient * reciprocal_distance * eigenbasis_projection).astype(jnp.bfloat16)
        vectors = radial_vectors.astype(jnp.float32)
        source_hat = jnp.einsum('pzr,ri->piz', forcing_contribution.astype(jnp.float32), vectors, precision=highest)
        flux_hat = jnp.einsum('pzr,ri->piz', axial_flux.astype(jnp.float32), vectors, precision=highest)
        combined = source_hat + jnp.einsum('pij,zj->piz', flux_hat, axial_matrix, precision=highest)
        coefficients = jnp.einsum('piz,zk->pik', combined, axial_vectors, precision=highest)
        coefficients = coefficients / (radial_values[None, :, None] + axial_eig[None, None, :] + HEAT_OFFSET)
        returned = jnp.einsum('pik,zk->piz', coefficients, axial_vectors, precision=highest)
        return jnp.einsum('piz,ri->pzr', returned, vectors, precision=highest)
    return lax.map(one_mode, (harmonic_amplitudes, radial_basis, radial_eig, mode_values))
```

```python
import functools
import math

import jax
import jax.numpy as jnp
from jax import lax
from jax.experimental import pallas as pl
from jax.experimental.pallas import tpu as pltpu
from jax.sharding import PartitionSpec as P


HEAT_OFFSET = 1.0
BF = jnp.bfloat16
F32 = jnp.float32


def wave_rows(first_mode, mode_count, first_angle, angle_count, circle):
    mode_ids = first_mode + jnp.arange(mode_count, dtype=jnp.int32)
    angle_ids = first_angle + jnp.arange(angle_count, dtype=jnp.int32)
    phase_index = mode_ids[:, None] * angle_ids[None, :] % circle
    angle_value = phase_index.astype(F32) * (2.0 * math.pi / circle)
    norm_factor = 1.0 / math.sqrt(circle)
    table = jnp.stack(
        [jnp.cos(angle_value) * norm_factor, -jnp.sin(angle_value) * norm_factor], axis=1
    )
    return table.astype(BF)


def chunk_count(modes):
    return max(c for c in range(1, 5) if modes % c == 0)


def round_up(value, unit):
    return -(-value // unit) * unit


def sums_kernel(modes, padded, vel_ref, adj_ref, div_ref, table_ref, scale_ref, *refs):
    *out_refs, field_s, sum_s = refs
    angles, block, radial = adj_ref.shape
    adj = adj_ref[...].astype(F32)
    for f in range(3):
        flux = (vel_ref[f].astype(F32) * adj).astype(BF)
        if f == 0:
            moved = lax.dot_general(
                flux.reshape(angles * block, radial),
                div_ref[...],
                (((1,), (1,)), ((), ())),
                preferred_element_type=F32,
            ).reshape(angles, block, radial)
            flux = (HEAT_OFFSET * adj + moved).astype(BF)
        field_s[f] = jnp.swapaxes(flux, 0, 1)

    def one(z, carry):
        heat, turn, flux = (
            jnp.dot(table_ref[...], field_s[f, z], preferred_element_type=F32) for f in range(3)
        )
        scale = scale_ref[...]
        sum_s[0, z] = heat[:padded] - scale * turn[padded:]
        sum_s[1, z] = flux[:padded]
        sum_s[2, z] = heat[padded:] + scale * turn[:padded]
        sum_s[3, z] = flux[padded:]
        return carry

    lax.fori_loop(0, block, one, 0)
    for k in range(4):
        turned = jnp.swapaxes(sum_s[k], 0, 1)
        step = modes // len(out_refs)
        for c, out_ref in enumerate(out_refs):
            out_ref[:, k // 2, k % 2] = turned[c * step : (c + 1) * step].astype(BF)


def azimuth_sums(velocity, adj_temp, radial_div, table, mode_values, reciprocal_distance, parts):
    modes = table.shape[0]
    angles, own_axial, radial = adj_temp.shape
    padded = round_up(modes, 8)
    block = 16 if own_axial % 16 == 0 else own_axial
    table = jnp.pad(jnp.moveaxis(table, 1, 0), ((0, 0), (0, padded - modes), (0, 0)))
    table = table.reshape(2 * padded, angles)
    scale = jnp.pad(
        mode_values[:, None] * reciprocal_distance[None], ((0, padded - modes), (0, 0))
    )
    flops = 2 * own_axial * radial * angles * (radial + 6 * padded)
    return pl.pallas_call(
        functools.partial(sums_kernel, modes, padded),
        grid=(own_axial // block,),
        in_specs=[
            pl.BlockSpec((3, angles, block, radial), lambda z: (0, 0, z, 0)),
            pl.BlockSpec((angles, block, radial), lambda z: (0, z, 0)),
            pl.BlockSpec((radial, radial), lambda z: (0, 0)),
            pl.BlockSpec((2 * padded, angles), lambda z: (0, 0)),
            pl.BlockSpec((padded, radial), lambda z: (0, 0)),
        ],
        out_specs=[
            pl.BlockSpec((modes // parts, 2, 2, block, radial), lambda z: (0, 0, 0, z, 0))
        ]
        * parts,
        out_shape=[jax.ShapeDtypeStruct((modes // parts, 2, 2, own_axial, radial), BF)] * parts,
        scratch_shapes=[
            pltpu.VMEM((3, block, angles, radial), BF),
            pltpu.VMEM((4, block, padded, radial), F32),
        ],
        compiler_params=pltpu.CompilerParams(vmem_limit_bytes=60 * 2**20),
        cost_estimate=pl.CostEstimate(
            flops=flops, bytes_accessed=8 * angles * own_axial * radial, transcendentals=0
        ),
        name="sums",
    )(velocity, adj_temp, radial_div, table, scale)


def radial_kernel(count, *refs):
    own_ref, others, basis_ref, out_ref = refs[0], refs[1:-2], refs[-2], refs[-1]
    radial = basis_ref.shape[1]
    for m in range(count):
        total = own_ref[m].astype(F32)
        for other in others:
            total = total + other[m].astype(F32)
        width = total.shape[0] * total.shape[1] * total.shape[2]
        hat = lax.dot_general(
            basis_ref[m],
            total.astype(BF).reshape(width, radial),
            (((0,), (1,)), ((), ())),
            preferred_element_type=F32,
        ).astype(BF)
        out_ref[:, m] = hat.reshape(out_ref.shape[0], out_ref.shape[2], width)


def radial_forward(own, others, basis, first, step, col_total):
    radial = basis.shape[1]
    width = 4 * own.shape[3]
    count = max(c for c in range(1, 8) if step % c == 0)
    skip = first // count
    field = (count, 2, 2, own.shape[3], radial)
    return pl.pallas_call(
        functools.partial(radial_kernel, count),
        grid=(step // count,),
        in_specs=[pl.BlockSpec(field, lambda m: (m, 0, 0, 0, 0)) for _ in (own, *others)]
        + [pl.BlockSpec((count, radial, radial), lambda m: (m + skip, 0, 0))],
        out_specs=pl.BlockSpec(
            (col_total, count, radial // col_total, width), lambda m: (0, m, 0, 0)
        ),
        out_shape=jax.ShapeDtypeStruct((col_total, step, radial // col_total, width), BF),
        compiler_params=pltpu.CompilerParams(vmem_limit_bytes=60 * 2**20),
        cost_estimate=pl.CostEstimate(
            flops=2 * step * radial * radial * width,
            bytes_accessed=2 * step * radial * (radial + 3 * width),
            transcendentals=0,
        ),
        name="radial",
    )(own, *others, basis)


def axial_kernel(lines_ref, forward_ref, basis_ref, radial_ref, axial_ref, out_ref):
    col_total, count, own_count, width = lines_ref.shape
    half = width // 2
    quarter = width // 4
    rows = count * own_count
    lines = jnp.concatenate(
        [
            jnp.concatenate(
                [
                    lines_ref[s, :, :, p * half : (p + 1) * half].reshape(rows, half)
                    for s in range(col_total)
                ],
                axis=1,
            )
            for p in range(2)
        ],
        axis=0,
    )
    coefficients = jnp.dot(lines, forward_ref[...], preferred_element_type=F32)
    eigen = radial_ref[...] + axial_ref[...] + HEAT_OFFSET
    coefficients = jnp.concatenate([coefficients[:rows] / eigen, coefficients[rows:] / eigen], axis=0)
    returned = lax.dot_general(
        coefficients.astype(BF),
        basis_ref[...],
        (((1,), (1,)), ((), ())),
        preferred_element_type=F32,
    )
    for s in range(col_total):
        own = slice(s * quarter, (s + 1) * quarter)
        pair = jnp.concatenate([returned[:rows, own], returned[rows:, own]], axis=1)
        out_ref[s] = pair.astype(BF).reshape(count, own_count, half)


def axial_solve(lines, forward, axial_basis, radial_values, axial_eig):
    col_total, step, own_count, width = lines.shape
    points = axial_basis.shape[0]
    count = max(c for c in range(1, 8) if step % c == 0)
    rows = step * own_count
    return pl.pallas_call(
        axial_kernel,
        grid=(step // count,),
        in_specs=[
            pl.BlockSpec((col_total, count, own_count, width), lambda m: (0, m, 0, 0)),
            pl.BlockSpec((2 * points, points), lambda m: (0, 0)),
            pl.BlockSpec((points, points), lambda m: (0, 0)),
            pl.BlockSpec((count * own_count, 1), lambda m: (m, 0)),
            pl.BlockSpec((1, points), lambda m: (0, 0)),
        ],
        out_specs=pl.BlockSpec((col_total, count, own_count, width // 2), lambda m: (0, m, 0, 0)),
        out_shape=jax.ShapeDtypeStruct((col_total, step, own_count, width // 2), BF),
        compiler_params=pltpu.CompilerParams(vmem_limit_bytes=60 * 2**20),
        cost_estimate=pl.CostEstimate(
            flops=12 * rows * points * points,
            bytes_accessed=6 * points * points + 6 * rows * points,
            transcendentals=0,
        ),
        name="axial",
    )(lines, forward, axial_basis, radial_values.reshape(rows, 1), axial_eig.reshape(1, points))


def last_kernel(count, returned_ref, basis_ref, *refs):
    out_ref = refs[-1]
    for m in range(count):
        lines = returned_ref[:, m]
        lines = lines.reshape(lines.shape[0] * lines.shape[1], lines.shape[2])
        out_ref[m] = lax.dot_general(
            lines, basis_ref[m], (((0,), (1,)), ((), ())), preferred_element_type=F32
        ).reshape(out_ref.shape[1:])


def radial_back(returned, basis, before, first):
    col_total, step, own_count, width = returned.shape
    modes, radial, _ = basis.shape
    count = max(c for c in range(1, 8) if step % c == 0)
    skip = first // count
    return pl.pallas_call(
        functools.partial(last_kernel, count),
        grid=(step // count,),
        in_specs=[
            pl.BlockSpec((col_total, count, own_count, width), lambda m: (0, m, 0, 0)),
            pl.BlockSpec((count, radial, radial), lambda m: (m + skip, 0, 0)),
        ]
        + [pl.BlockSpec(memory_space=pl.ANY) for _ in before],
        out_specs=pl.BlockSpec((count, 2, width // 2, radial), lambda m: (m + skip, 0, 0, 0)),
        out_shape=jax.ShapeDtypeStruct((modes, 2, width // 2, radial), F32),
        input_output_aliases={2: 0} if before else {},
        compiler_params=pltpu.CompilerParams(vmem_limit_bytes=60 * 2**20),
        cost_estimate=pl.CostEstimate(
            flops=2 * step * radial * radial * width,
            bytes_accessed=2 * step * radial * (radial + 3 * width),
            transcendentals=0,
        ),
        name="last",
    )(returned, basis, *before)


def body(
    velocity,
    adj_temp,
    radial_div,
    reciprocal_distance,
    radial_basis,
    radial_eig,
    axial_diff,
    axial_basis,
    axial_eig,
):
    row_total = lax.axis_size("row")
    col_total = lax.axis_size("col")
    row_place = lax.axis_index("row")
    col_place = lax.axis_index("col")
    modes = radial_basis.shape[0]
    angles, own_axial, radial_points = adj_temp.shape
    axial_points = axial_basis.shape[0]
    own_count = radial_points // col_total
    circle = angles * row_total
    parts = chunk_count(modes)
    step = modes // parts

    def partial_sums(place):
        table = wave_rows(place * modes, modes, row_place * angles, angles, circle)
        mode_values = (place * modes + jnp.arange(modes, dtype=jnp.int32)).astype(F32)
        return azimuth_sums(
            velocity, adj_temp, radial_div, table, mode_values, reciprocal_distance, parts
        )

    arrived = [[] for _ in range(parts)]
    for shift in range(1, row_total):
        sums = partial_sums((row_place + shift) % row_total)
        pairs = [(a, (a + shift) % row_total) for a in range(row_total)]
        for c in range(parts):
            arrived[c].append(lax.ppermute(sums[c], "row", pairs))
    own = partial_sums(row_place)

    returning = jnp.einsum("zj,zk->jk", axial_diff, axial_basis, preferred_element_type=F32)
    forward = jnp.stack(
        [
            axial_basis.reshape(col_total, own_axial, axial_points),
            returning.astype(BF).reshape(col_total, own_axial, axial_points),
        ],
        axis=1,
    )
    axial_blocks = axial_basis.reshape(col_total, own_axial, axial_points)
    radial_values = lax.dynamic_slice_in_dim(radial_eig, col_place * own_count, own_count, 1)

    fits = own_axial % 64 == 0 and own_count % 16 == 0
    outs = []
    new_temp = ()
    for c in range(parts):
        part = slice(c * step, (c + 1) * step)
        hat = radial_forward(own[c], arrived[c], radial_basis, c * step, step, col_total)
        lines = lax.all_to_all(hat, "col", split_axis=0, concat_axis=0, tiled=True)
        if fits:
            returned = axial_solve(
                lines,
                forward.reshape(2 * axial_points, axial_points),
                axial_basis,
                radial_values[part],
                axial_eig,
            )
        else:
            lines = lines.reshape(col_total, step, own_count, 2, 2, own_axial)
            coefficients = jnp.einsum(
                "smxpfy,sfyk->pmxk", lines, forward, preferred_element_type=F32
            )
            coefficients = coefficients / (
                radial_values[part][None, :, :, None] + axial_eig + HEAT_OFFSET
            )
            returned = jnp.einsum(
                "pmxk,syk->smxpy", coefficients.astype(BF), axial_blocks, preferred_element_type=F32
            ).astype(BF)
            returned = returned.reshape(col_total, step, own_count, 2 * own_axial)
        returned = lax.all_to_all(returned, "col", split_axis=0, concat_axis=0, tiled=True)
        if fits:
            new_temp = (radial_back(returned, radial_basis, new_temp, c * step),)
            continue
        returned = jnp.moveaxis(returned, 0, 1).reshape(step, radial_points, 2 * own_axial)
        outs.append(
            jnp.einsum("miw,mri->mwr", returned, radial_basis[part], preferred_element_type=F32).reshape(
                step, 2, own_axial, radial_points
            )
        )
    return new_temp[0] if fits else jnp.concatenate(outs, axis=0)


def both_sums_kernel(modes, padded, vel_ref, adj_ref, div_ref, table_ref, scale_ref, *refs):
    *out_refs, field_s, sum_s = refs
    angles, block, radial = adj_ref.shape
    adj = adj_ref[...].astype(F32)
    for f in range(3):
        flux = (vel_ref[f].astype(F32) * adj).astype(BF)
        if f == 0:
            moved = lax.dot_general(
                flux.reshape(angles * block, radial),
                div_ref[...],
                (((1,), (1,)), ((), ())),
                preferred_element_type=F32,
            ).reshape(angles, block, radial)
            flux = (HEAT_OFFSET * adj + moved).astype(BF)
        field_s[f] = jnp.swapaxes(flux, 0, 1)

    def one(z, carry):
        heat, turn, flux = (
            jnp.dot(table_ref[...], field_s[f, z], preferred_element_type=F32) for f in range(3)
        )
        for d in range(len(out_refs)):
            re = slice(2 * d * padded, (2 * d + 1) * padded)
            im = slice((2 * d + 1) * padded, (2 * d + 2) * padded)
            scale = scale_ref[d]
            sum_s[4 * d, z] = heat[re] - scale * turn[im]
            sum_s[4 * d + 1, z] = flux[re]
            sum_s[4 * d + 2, z] = heat[im] + scale * turn[re]
            sum_s[4 * d + 3, z] = flux[im]
        return carry

    lax.fori_loop(0, block, one, 0)
    for d, out_ref in enumerate(out_refs):
        for k in range(4):
            turned = jnp.swapaxes(sum_s[4 * d + k], 0, 1)
            out_ref[:, k // 2, k % 2] = turned[:modes].astype(BF)


def both_sums(velocity, adj_temp, radial_div, tables, mode_values, reciprocal_distance):
    dests, modes = mode_values.shape
    angles, own_axial, radial = adj_temp.shape
    padded = round_up(modes, 8)
    block = 16 if own_axial % 16 == 0 else own_axial
    table = jnp.pad(jnp.moveaxis(tables, 2, 1), ((0, 0), (0, 0), (0, padded - modes), (0, 0)))
    table = table.reshape(dests * 2 * padded, angles)
    scale = mode_values[:, :, None] * reciprocal_distance[None, None]
    scale = jnp.pad(scale, ((0, 0), (0, padded - modes), (0, 0)))
    flops = 2 * own_axial * radial * angles * (radial + 6 * padded * dests)
    return pl.pallas_call(
        functools.partial(both_sums_kernel, modes, padded),
        grid=(own_axial // block,),
        in_specs=[
            pl.BlockSpec((3, angles, block, radial), lambda z: (0, 0, z, 0)),
            pl.BlockSpec((angles, block, radial), lambda z: (0, z, 0)),
            pl.BlockSpec((radial, radial), lambda z: (0, 0)),
            pl.BlockSpec((dests * 2 * padded, angles), lambda z: (0, 0)),
            pl.BlockSpec((dests, padded, radial), lambda z: (0, 0, 0)),
        ],
        out_specs=[pl.BlockSpec((modes, 2, 2, block, radial), lambda z: (0, 0, 0, z, 0))] * dests,
        out_shape=[jax.ShapeDtypeStruct((modes, 2, 2, own_axial, radial), BF)] * dests,
        scratch_shapes=[
            pltpu.VMEM((3, block, angles, radial), BF),
            pltpu.VMEM((4 * dests, block, padded, radial), F32),
        ],
        compiler_params=pltpu.CompilerParams(vmem_limit_bytes=60 * 2**20),
        cost_estimate=pl.CostEstimate(
            flops=flops, bytes_accessed=8 * angles * own_axial * radial, transcendentals=0
        ),
        name="sums",
    )(velocity, adj_temp, radial_div, table, scale)


MESH = pl.DeviceIdType.MESH


def solve_kernel(
    chunks,
    lags,
    own_hbm,
    other_hbm,
    basis_hbm,
    forward_ref,
    back_ref,
    radial_ref,
    axial_ref,
    out_hbm,
    field_s,
    lines_s,
    cross_s,
    back_s,
    part_s,
    cross_o,
    back_o,
    own_s,
    basis_s,
    again_s,
    out_s,
    row_send,
    row_recv,
    ahead_send,
    ahead_recv,
    cross_send,
    cross_recv,
    back_send,
    back_recv,
    load_sem,
    out_sem,
):
    group, modes, block, width = lines_s.shape
    count = modes // chunks
    half = width // 2
    quarter = width // 4
    rows = count * block
    lag_axial, lag_add, lag_last = lags
    row_place = lax.axis_index("row")
    col_place = lax.axis_index("col")
    side = col_place // group
    place = col_place % group
    across = {"row": 1 - row_place}
    mirror = {"col": (1 - side) * group + place}

    def peer(k):
        return (place + k) % group

    def peer_id(k):
        return {"col": side * group + peer(k)}

    def span(c):
        return pl.ds(c * count, count)

    def row_copy(c):
        return pltpu.make_async_remote_copy(
            src_ref=other_hbm.at[span(c)],
            dst_ref=field_s.at[span(c)],
            send_sem=row_send.at[c],
            recv_sem=row_recv.at[c],
            device_id=across,
            device_id_type=MESH,
        )

    def ahead_copy(c, k):
        first = pl.multiple_of(peer(k) * block, block)
        return pltpu.make_async_remote_copy(
            src_ref=field_s.at[span(c), pl.ds(first, block)],
            dst_ref=lines_s.at[place, span(c)],
            send_sem=ahead_send.at[c % 2, k],
            recv_sem=ahead_recv.at[c, k],
            device_id=peer_id(k),
            device_id_type=MESH,
        )

    def cross_copy(c):
        return pltpu.make_async_remote_copy(
            src_ref=cross_o.at[c % 2],
            dst_ref=cross_s.at[c],
            send_sem=cross_send.at[c % 2],
            recv_sem=cross_recv.at[c],
            device_id=mirror,
            device_id_type=MESH,
        )

    def back_copy(c, k):
        return pltpu.make_async_remote_copy(
            src_ref=back_o.at[c % 2, peer(k)],
            dst_ref=back_s.at[place, span(c)],
            send_sem=back_send.at[c % 2, k],
            recv_sem=back_recv.at[c, k],
            device_id=peer_id(k),
            device_id_type=MESH,
        )

    def own_load(c):
        return pltpu.make_async_copy(own_hbm.at[span(c)], own_s.at[c % 2], load_sem.at[0, c % 2])

    def basis_load(c):
        return pltpu.make_async_copy(basis_hbm.at[span(c)], basis_s.at[c % 2], load_sem.at[1, c % 2])

    def again_load(c):
        return pltpu.make_async_copy(basis_hbm.at[span(c)], again_s.at[c % 2], load_sem.at[2, c % 2])

    def out_copy(c):
        return pltpu.make_async_copy(out_s.at[c % 2], out_hbm.at[span(c)], out_sem.at[c % 2])

    others = range(1, group)
    own_load(0).start()
    basis_load(0).start()
    again_load(0).start()
    barrier = pltpu.get_barrier_semaphore()
    for device in [across, mirror] + [peer_id(k) for k in others]:
        pl.semaphore_signal(barrier, inc=1, device_id=device, device_id_type=MESH)
    pl.semaphore_wait(barrier, group + 1)

    def send_row(c, carry):
        row_copy(c).start()
        return carry

    lax.fori_loop(0, chunks, send_row, 0)

    def radial_part(c):
        own_load(c).wait()
        basis_load(c).wait()

        @pl.when(c + 1 < chunks)
        def _():
            own_load(c + 1).start()
            basis_load(c + 1).start()

        @pl.when(c >= 2)
        def _():
            for k in others:
                ahead_copy(c - 2, k).wait_send()

        row_copy(c).wait_recv()
        for m in range(count):
            mode = c * count + m
            total = own_s[c % 2, m].astype(F32) + field_s[mode].astype(F32)
            hat = lax.dot_general(
                basis_s[c % 2, m],
                total.astype(BF),
                (((0,), (1,)), ((), ())),
                preferred_element_type=F32,
            )
            field_s[mode] = hat.astype(BF)
        mine = pl.multiple_of(place * block, block)
        lines_s[place, span(c)] = field_s[span(c), pl.ds(mine, block), :]
        for k in others:
            ahead_copy(c, k).start()

    def axial_part(c):
        for k in others:
            ahead_copy(c, k).wait_recv()

        @pl.when(c >= 2)
        def _():
            cross_copy(c - 2).wait_send()

        first = pl.multiple_of(c * rows, rows)
        eigen = radial_ref[pl.ds(first, rows), :] + axial_ref[...] + HEAT_OFFSET
        returned = []
        for p in range(2):
            lines = jnp.concatenate(
                [
                    lines_s[s, span(c), :, p * half : (p + 1) * half].reshape(rows, half)
                    for s in range(group)
                ],
                axis=1,
            )
            coefficients = jnp.dot(lines, forward_ref[...], preferred_element_type=F32) / eigen
            returned.append(
                lax.dot_general(
                    coefficients.astype(BF),
                    back_ref[...],
                    (((1,), (1,)), ((), ())),
                    preferred_element_type=F32,
                )
            )
        for s in range(2 * group):
            own = slice(s * quarter, (s + 1) * quarter)
            pair = jnp.concatenate([returned[0][:, own], returned[1][:, own]], axis=1)
            pair = pair.reshape(count, block, half)
            if s < group:
                part_s[c % part_s.shape[0], s] = pair
            else:
                cross_o[c % 2, s - group] = pair.astype(BF)
        cross_copy(c).start()

    def add_part(c):
        cross_copy(c).wait_recv()

        @pl.when(c >= 2)
        def _():
            for k in others:
                back_copy(c - 2, k).wait_send()

        total = part_s[c % part_s.shape[0]] + cross_s[c].astype(F32)
        back_o[c % 2] = total.astype(BF)
        back_s[place, span(c)] = back_o[c % 2, place]
        for k in others:
            back_copy(c, k).start()

    def last_part(c):
        again_load(c).wait()

        @pl.when(c + 1 < chunks)
        def _():
            again_load(c + 1).start()

        @pl.when(c >= 2)
        def _():
            out_copy(c - 2).wait()

        for k in others:
            back_copy(c, k).wait_recv()
        for m in range(count):
            lines = back_s[:, c * count + m].reshape(group * block, half)
            out_s[c % 2, m] = lax.dot_general(
                lines, again_s[c % 2, m], (((0,), (1,)), ((), ())), preferred_element_type=F32
            ).reshape(out_s.shape[2:])
        out_copy(c).start()

    def step(s, carry):
        for part, lag in (
            (radial_part, 0),
            (add_part, lag_add),
            (axial_part, lag_axial),
            (last_part, lag_last),
        ):
            pl.when((s >= lag) & (s < chunks + lag))(functools.partial(part, s - lag))
        return carry

    lax.fori_loop(0, chunks + lag_last, step, 0)

    def row_done(c, carry):
        row_copy(c).wait_send()
        return carry

    lax.fori_loop(0, chunks, row_done, 0)
    for c in range(chunks - 2, chunks):
        for k in others:
            ahead_copy(c, k).wait_send()
            back_copy(c, k).wait_send()
        cross_copy(c).wait_send()
        out_copy(c).wait()


def solve(own, other, basis, forward, back, radial_values, axial_eig, group, chunks, lags):
    modes, radial, _ = basis.shape
    width = own.shape[1]
    points = forward.shape[1]
    block = radial // group
    count = modes // chunks
    half = width // 2
    anywhere = pl.BlockSpec(memory_space=pl.ANY)
    vmem = pl.BlockSpec(memory_space=pltpu.VMEM)
    own_axial = width // 4
    dma = pltpu.SemaphoreType.DMA
    lines = 2 * modes * block
    sent = 2 * modes * radial * width * 3
    return pl.pallas_call(
        functools.partial(solve_kernel, chunks, lags),
        in_specs=[anywhere] * 3 + [vmem] * 4,
        out_specs=anywhere,
        out_shape=jax.ShapeDtypeStruct((modes, 2, own_axial, radial), F32),
        scratch_shapes=[
            pltpu.VMEM((modes, width, radial), BF),
            pltpu.VMEM((group, modes, block, width), BF),
            pltpu.VMEM((chunks, group, count, block, half), BF),
            pltpu.VMEM((group, modes, block, half), BF),
            pltpu.VMEM((lags[1] - lags[0], group, count, block, half), F32),
            pltpu.VMEM((2, group, count, block, half), BF),
            pltpu.VMEM((2, group, count, block, half), BF),
            pltpu.VMEM((2, count, width, radial), BF),
            pltpu.VMEM((2, count, radial, radial), BF),
            pltpu.VMEM((2, count, radial, radial), BF),
            pltpu.VMEM((2, count, 2, own_axial, radial), F32),
            dma((chunks,)),
            dma((chunks,)),
            dma((2, group)),
            dma((chunks, group)),
            dma((2,)),
            dma((chunks,)),
            dma((2, group)),
            dma((chunks, group)),
            dma((3, 2)),
            dma((2,)),
        ],
        compiler_params=pltpu.CompilerParams(
            collective_id=0, has_side_effects=True, vmem_limit_bytes=63 * 2**20
        ),
        cost_estimate=pl.CostEstimate(
            flops=4 * lines * points * points + 6 * modes * radial * radial * width,
            bytes_accessed=sent,
            transcendentals=0,
        ),
        name="solve",
    )(own, other, basis, forward, back, radial_values.reshape(modes * block, 1), axial_eig[None])


CHUNK_MODES = 7
LAGS = (1, 2, 3)


def fused_body(
    velocity,
    adj_temp,
    radial_div,
    reciprocal_distance,
    radial_basis,
    radial_eig,
    axial_diff,
    axial_basis,
    axial_eig,
):
    row_total = lax.axis_size("row")
    group = lax.axis_size("col") // 2
    row_place = lax.axis_index("row")
    col_place = lax.axis_index("col")
    side, place = col_place // group, col_place % group
    modes = radial_basis.shape[0]
    angles, own_axial, radial_points = adj_temp.shape
    axial_points = axial_basis.shape[0]
    circle = angles * row_total
    block = radial_points // group
    dests = (row_place, 1 - row_place)
    tables = jnp.stack(
        [wave_rows(d * modes, modes, row_place * angles, angles, circle) for d in dests]
    )
    mode_values = jnp.stack(
        [(d * modes + jnp.arange(modes, dtype=jnp.int32)).astype(F32) for d in dests]
    )
    own, other = both_sums(
        velocity, adj_temp, radial_div, tables, mode_values, reciprocal_distance
    )
    own = own.reshape(modes, 4 * own_axial, radial_points)
    other = other.reshape(modes, 4 * own_axial, radial_points)

    half_points = axial_points // 2
    near = lax.dynamic_slice_in_dim(axial_basis, side * half_points, half_points, 0)
    far = lax.dynamic_slice_in_dim(axial_basis, (1 - side) * half_points, half_points, 0)
    near_diff = lax.dynamic_slice_in_dim(axial_diff, side * half_points, half_points, 1)
    turned = jnp.einsum("zj,zk->jk", near_diff, axial_basis, preferred_element_type=F32).astype(BF)
    forward = jnp.stack(
        [x.reshape(group, own_axial, axial_points) for x in (near, turned)], axis=1
    ).reshape(axial_points, axial_points)
    back = jnp.concatenate([near, far], axis=0)
    radial_values = lax.dynamic_slice_in_dim(radial_eig, place * block, block, 1)
    chunks = modes // CHUNK_MODES
    return solve(
        own, other, radial_basis, forward, back, radial_values, axial_eig, group, chunks, LAGS
    )


def solution(mesh):
    in_specs = (
        P(None, "row", "col", None),
        P("row", "col", None),
        P(),
        P(),
        P("row", None, None),
        P("row", None),
        P(),
        P(),
        P(),
    )
    out_specs = P("row", None, "col", None)
    if mesh.shape["row"] == 2 and mesh.shape["col"] == 16:
        return jax.shard_map(
            fused_body, mesh=mesh, in_specs=in_specs, out_specs=out_specs, check_vma=False
        )
    return jax.shard_map(body, mesh=mesh, in_specs=in_specs, out_specs=out_specs, check_vma=False)
```

```python
import functools
import math

import jax
import jax.numpy as jnp
from jax import lax
from jax.experimental import pallas as pl
from jax.experimental.pallas import tpu as pltpu
from jax.sharding import PartitionSpec as P


HEAT_OFFSET = 1.0
BF = jnp.bfloat16
F32 = jnp.float32


def wave_rows(first_mode, mode_count, first_angle, angle_count, circle):
    mode_ids = first_mode + jnp.arange(mode_count, dtype=jnp.int32)
    angle_ids = first_angle + jnp.arange(angle_count, dtype=jnp.int32)
    phase_index = mode_ids[:, None] * angle_ids[None, :] % circle
    angle_value = phase_index.astype(F32) * (2.0 * math.pi / circle)
    norm_factor = 1.0 / math.sqrt(circle)
    table = jnp.stack(
        [jnp.cos(angle_value) * norm_factor, -jnp.sin(angle_value) * norm_factor], axis=1
    )
    return table.astype(BF)


def chunk_count(modes):
    return max(c for c in range(1, 5) if modes % c == 0)


def round_up(value, unit):
    return -(-value // unit) * unit


def sums_kernel(modes, padded, vel_ref, adj_ref, div_ref, table_ref, scale_ref, *refs):
    *out_refs, field_s, sum_s = refs
    angles, block, radial = adj_ref.shape
    adj = adj_ref[...].astype(F32)
    for f in range(3):
        flux = (vel_ref[f].astype(F32) * adj).astype(BF)
        if f == 0:
            moved = lax.dot_general(
                flux.reshape(angles * block, radial),
                div_ref[...],
                (((1,), (1,)), ((), ())),
                preferred_element_type=F32,
            ).reshape(angles, block, radial)
            flux = (HEAT_OFFSET * adj + moved).astype(BF)
        field_s[f] = jnp.swapaxes(flux, 0, 1)

    def one(z, carry):
        heat, turn, flux = (
            jnp.dot(table_ref[...], field_s[f, z], preferred_element_type=F32) for f in range(3)
        )
        scale = scale_ref[...]
        sum_s[0, z] = heat[:padded] - scale * turn[padded:]
        sum_s[1, z] = flux[:padded]
        sum_s[2, z] = heat[padded:] + scale * turn[:padded]
        sum_s[3, z] = flux[padded:]
        return carry

    lax.fori_loop(0, block, one, 0)
    for k in range(4):
        turned = jnp.swapaxes(sum_s[k], 0, 1)
        step = modes // len(out_refs)
        for c, out_ref in enumerate(out_refs):
            out_ref[:, k // 2, k % 2] = turned[c * step : (c + 1) * step].astype(BF)


def azimuth_sums(velocity, adj_temp, radial_div, table, mode_values, reciprocal_distance, parts):
    modes = table.shape[0]
    angles, own_axial, radial = adj_temp.shape
    padded = round_up(modes, 8)
    block = 16 if own_axial % 16 == 0 else own_axial
    table = jnp.pad(jnp.moveaxis(table, 1, 0), ((0, 0), (0, padded - modes), (0, 0)))
    table = table.reshape(2 * padded, angles)
    scale = jnp.pad(
        mode_values[:, None] * reciprocal_distance[None], ((0, padded - modes), (0, 0))
    )
    flops = 2 * own_axial * radial * angles * (radial + 6 * padded)
    return pl.pallas_call(
        functools.partial(sums_kernel, modes, padded),
        grid=(own_axial // block,),
        in_specs=[
            pl.BlockSpec((3, angles, block, radial), lambda z: (0, 0, z, 0)),
            pl.BlockSpec((angles, block, radial), lambda z: (0, z, 0)),
            pl.BlockSpec((radial, radial), lambda z: (0, 0)),
            pl.BlockSpec((2 * padded, angles), lambda z: (0, 0)),
            pl.BlockSpec((padded, radial), lambda z: (0, 0)),
        ],
        out_specs=[
            pl.BlockSpec((modes // parts, 2, 2, block, radial), lambda z: (0, 0, 0, z, 0))
        ]
        * parts,
        out_shape=[jax.ShapeDtypeStruct((modes // parts, 2, 2, own_axial, radial), BF)] * parts,
        scratch_shapes=[
            pltpu.VMEM((3, block, angles, radial), BF),
            pltpu.VMEM((4, block, padded, radial), F32),
        ],
        compiler_params=pltpu.CompilerParams(vmem_limit_bytes=60 * 2**20),
        cost_estimate=pl.CostEstimate(
            flops=flops, bytes_accessed=8 * angles * own_axial * radial, transcendentals=0
        ),
        name="sums",
    )(velocity, adj_temp, radial_div, table, scale)


def radial_kernel(count, *refs):
    own_ref, others, basis_ref, out_ref = refs[0], refs[1:-2], refs[-2], refs[-1]
    radial = basis_ref.shape[1]
    for m in range(count):
        total = own_ref[m].astype(F32)
        for other in others:
            total = total + other[m].astype(F32)
        width = total.shape[0] * total.shape[1] * total.shape[2]
        hat = lax.dot_general(
            basis_ref[m],
            total.astype(BF).reshape(width, radial),
            (((0,), (1,)), ((), ())),
            preferred_element_type=F32,
        ).astype(BF)
        out_ref[:, m] = hat.reshape(out_ref.shape[0], out_ref.shape[2], width)


def radial_forward(own, others, basis, first, step, col_total):
    radial = basis.shape[1]
    width = 4 * own.shape[3]
    count = max(c for c in range(1, 8) if step % c == 0)
    skip = first // count
    field = (count, 2, 2, own.shape[3], radial)
    return pl.pallas_call(
        functools.partial(radial_kernel, count),
        grid=(step // count,),
        in_specs=[pl.BlockSpec(field, lambda m: (m, 0, 0, 0, 0)) for _ in (own, *others)]
        + [pl.BlockSpec((count, radial, radial), lambda m: (m + skip, 0, 0))],
        out_specs=pl.BlockSpec(
            (col_total, count, radial // col_total, width), lambda m: (0, m, 0, 0)
        ),
        out_shape=jax.ShapeDtypeStruct((col_total, step, radial // col_total, width), BF),
        compiler_params=pltpu.CompilerParams(vmem_limit_bytes=60 * 2**20),
        cost_estimate=pl.CostEstimate(
            flops=2 * step * radial * radial * width,
            bytes_accessed=2 * step * radial * (radial + 3 * width),
            transcendentals=0,
        ),
        name="radial",
    )(own, *others, basis)


def axial_kernel(lines_ref, forward_ref, basis_ref, radial_ref, axial_ref, out_ref):
    col_total, count, own_count, width = lines_ref.shape
    half = width // 2
    quarter = width // 4
    rows = count * own_count
    lines = jnp.concatenate(
        [
            jnp.concatenate(
                [
                    lines_ref[s, :, :, p * half : (p + 1) * half].reshape(rows, half)
                    for s in range(col_total)
                ],
                axis=1,
            )
            for p in range(2)
        ],
        axis=0,
    )
    coefficients = jnp.dot(lines, forward_ref[...], preferred_element_type=F32)
    eigen = radial_ref[...] + axial_ref[...] + HEAT_OFFSET
    coefficients = jnp.concatenate([coefficients[:rows] / eigen, coefficients[rows:] / eigen], axis=0)
    returned = lax.dot_general(
        coefficients.astype(BF),
        basis_ref[...],
        (((1,), (1,)), ((), ())),
        preferred_element_type=F32,
    )
    for s in range(col_total):
        own = slice(s * quarter, (s + 1) * quarter)
        pair = jnp.concatenate([returned[:rows, own], returned[rows:, own]], axis=1)
        out_ref[s] = pair.astype(BF).reshape(count, own_count, half)


def axial_solve(lines, forward, axial_basis, radial_values, axial_eig):
    col_total, step, own_count, width = lines.shape
    points = axial_basis.shape[0]
    count = max(c for c in range(1, 8) if step % c == 0)
    rows = step * own_count
    return pl.pallas_call(
        axial_kernel,
        grid=(step // count,),
        in_specs=[
            pl.BlockSpec((col_total, count, own_count, width), lambda m: (0, m, 0, 0)),
            pl.BlockSpec((2 * points, points), lambda m: (0, 0)),
            pl.BlockSpec((points, points), lambda m: (0, 0)),
            pl.BlockSpec((count * own_count, 1), lambda m: (m, 0)),
            pl.BlockSpec((1, points), lambda m: (0, 0)),
        ],
        out_specs=pl.BlockSpec((col_total, count, own_count, width // 2), lambda m: (0, m, 0, 0)),
        out_shape=jax.ShapeDtypeStruct((col_total, step, own_count, width // 2), BF),
        compiler_params=pltpu.CompilerParams(vmem_limit_bytes=60 * 2**20),
        cost_estimate=pl.CostEstimate(
            flops=12 * rows * points * points,
            bytes_accessed=6 * points * points + 6 * rows * points,
            transcendentals=0,
        ),
        name="axial",
    )(lines, forward, axial_basis, radial_values.reshape(rows, 1), axial_eig.reshape(1, points))


def last_kernel(count, returned_ref, basis_ref, *refs):
    out_ref = refs[-1]
    for m in range(count):
        lines = returned_ref[:, m]
        lines = lines.reshape(lines.shape[0] * lines.shape[1], lines.shape[2])
        out_ref[m] = lax.dot_general(
            lines, basis_ref[m], (((0,), (1,)), ((), ())), preferred_element_type=F32
        ).reshape(out_ref.shape[1:])


def radial_back(returned, basis, before, first):
    col_total, step, own_count, width = returned.shape
    modes, radial, _ = basis.shape
    count = max(c for c in range(1, 8) if step % c == 0)
    skip = first // count
    return pl.pallas_call(
        functools.partial(last_kernel, count),
        grid=(step // count,),
        in_specs=[
            pl.BlockSpec((col_total, count, own_count, width), lambda m: (0, m, 0, 0)),
            pl.BlockSpec((count, radial, radial), lambda m: (m + skip, 0, 0)),
        ]
        + [pl.BlockSpec(memory_space=pl.ANY) for _ in before],
        out_specs=pl.BlockSpec((count, 2, width // 2, radial), lambda m: (m + skip, 0, 0, 0)),
        out_shape=jax.ShapeDtypeStruct((modes, 2, width // 2, radial), F32),
        input_output_aliases={2: 0} if before else {},
        compiler_params=pltpu.CompilerParams(vmem_limit_bytes=60 * 2**20),
        cost_estimate=pl.CostEstimate(
            flops=2 * step * radial * radial * width,
            bytes_accessed=2 * step * radial * (radial + 3 * width),
            transcendentals=0,
        ),
        name="last",
    )(returned, basis, *before)


def body(
    velocity,
    adj_temp,
    radial_div,
    reciprocal_distance,
    radial_basis,
    radial_eig,
    axial_diff,
    axial_basis,
    axial_eig,
):
    row_total = lax.axis_size("row")
    col_total = lax.axis_size("col")
    row_place = lax.axis_index("row")
    col_place = lax.axis_index("col")
    modes = radial_basis.shape[0]
    angles, own_axial, radial_points = adj_temp.shape
    axial_points = axial_basis.shape[0]
    own_count = radial_points // col_total
    circle = angles * row_total
    parts = chunk_count(modes)
    step = modes // parts

    def partial_sums(place):
        table = wave_rows(place * modes, modes, row_place * angles, angles, circle)
        mode_values = (place * modes + jnp.arange(modes, dtype=jnp.int32)).astype(F32)
        return azimuth_sums(
            velocity, adj_temp, radial_div, table, mode_values, reciprocal_distance, parts
        )

    arrived = [[] for _ in range(parts)]
    for shift in range(1, row_total):
        sums = partial_sums((row_place + shift) % row_total)
        pairs = [(a, (a + shift) % row_total) for a in range(row_total)]
        for c in range(parts):
            arrived[c].append(lax.ppermute(sums[c], "row", pairs))
    own = partial_sums(row_place)

    returning = jnp.einsum("zj,zk->jk", axial_diff, axial_basis, preferred_element_type=F32)
    forward = jnp.stack(
        [
            axial_basis.reshape(col_total, own_axial, axial_points),
            returning.astype(BF).reshape(col_total, own_axial, axial_points),
        ],
        axis=1,
    )
    axial_blocks = axial_basis.reshape(col_total, own_axial, axial_points)
    radial_values = lax.dynamic_slice_in_dim(radial_eig, col_place * own_count, own_count, 1)

    fits = own_axial % 64 == 0 and own_count % 16 == 0
    outs = []
    new_temp = ()
    for c in range(parts):
        part = slice(c * step, (c + 1) * step)
        hat = radial_forward(own[c], arrived[c], radial_basis, c * step, step, col_total)
        lines = lax.all_to_all(hat, "col", split_axis=0, concat_axis=0, tiled=True)
        if fits:
            returned = axial_solve(
                lines,
                forward.reshape(2 * axial_points, axial_points),
                axial_basis,
                radial_values[part],
                axial_eig,
            )
        else:
            lines = lines.reshape(col_total, step, own_count, 2, 2, own_axial)
            coefficients = jnp.einsum(
                "smxpfy,sfyk->pmxk", lines, forward, preferred_element_type=F32
            )
            coefficients = coefficients / (
                radial_values[part][None, :, :, None] + axial_eig + HEAT_OFFSET
            )
            returned = jnp.einsum(
                "pmxk,syk->smxpy", coefficients.astype(BF), axial_blocks, preferred_element_type=F32
            ).astype(BF)
            returned = returned.reshape(col_total, step, own_count, 2 * own_axial)
        returned = lax.all_to_all(returned, "col", split_axis=0, concat_axis=0, tiled=True)
        if fits:
            new_temp = (radial_back(returned, radial_basis, new_temp, c * step),)
            continue
        returned = jnp.moveaxis(returned, 0, 1).reshape(step, radial_points, 2 * own_axial)
        outs.append(
            jnp.einsum("miw,mri->mwr", returned, radial_basis[part], preferred_element_type=F32).reshape(
                step, 2, own_axial, radial_points
            )
        )
    return new_temp[0] if fits else jnp.concatenate(outs, axis=0)


def both_sums_kernel(modes, padded, vel_ref, adj_ref, div_ref, table_ref, scale_ref, *refs):
    *out_refs, field_s, sum_s = refs
    angles, block, radial = adj_ref.shape
    adj = adj_ref[...].astype(F32)
    for f in range(3):
        flux = (vel_ref[f].astype(F32) * adj).astype(BF)
        if f == 0:
            moved = lax.dot_general(
                flux.reshape(angles * block, radial),
                div_ref[...],
                (((1,), (1,)), ((), ())),
                preferred_element_type=F32,
            ).reshape(angles, block, radial)
            flux = (HEAT_OFFSET * adj + moved).astype(BF)
        field_s[f] = jnp.swapaxes(flux, 0, 1)

    def one(z, carry):
        heat, turn, flux = (
            jnp.dot(table_ref[...], field_s[f, z], preferred_element_type=F32) for f in range(3)
        )
        for d in range(len(out_refs)):
            re = slice(2 * d * padded, (2 * d + 1) * padded)
            im = slice((2 * d + 1) * padded, (2 * d + 2) * padded)
            scale = scale_ref[d]
            sum_s[4 * d, z] = heat[re] - scale * turn[im]
            sum_s[4 * d + 1, z] = flux[re]
            sum_s[4 * d + 2, z] = heat[im] + scale * turn[re]
            sum_s[4 * d + 3, z] = flux[im]
        return carry

    lax.fori_loop(0, block, one, 0)
    for d, out_ref in enumerate(out_refs):
        for k in range(4):
            turned = jnp.swapaxes(sum_s[4 * d + k], 0, 1)
            out_ref[:, k // 2, k % 2] = turned[:modes].astype(BF)


def both_sums(
    velocity, adj_temp, radial_div, tables, mode_values, reciprocal_distance, modes
):
    dests, padded = mode_values.shape
    angles, own_axial, radial = adj_temp.shape
    block = 16 if own_axial % 16 == 0 else own_axial
    table = jnp.moveaxis(tables, 2, 1).reshape(dests * 2 * padded, angles)
    scale = mode_values[:, :, None] * reciprocal_distance[None, None]
    flops = 2 * own_axial * radial * angles * (radial + 6 * padded * dests)
    return pl.pallas_call(
        functools.partial(both_sums_kernel, modes, padded),
        grid=(own_axial // block,),
        in_specs=[
            pl.BlockSpec((3, angles, block, radial), lambda z: (0, 0, z, 0)),
            pl.BlockSpec((angles, block, radial), lambda z: (0, z, 0)),
            pl.BlockSpec((radial, radial), lambda z: (0, 0)),
            pl.BlockSpec((dests * 2 * padded, angles), lambda z: (0, 0)),
            pl.BlockSpec((dests, padded, radial), lambda z: (0, 0, 0)),
        ],
        out_specs=[pl.BlockSpec((modes, 2, 2, block, radial), lambda z: (0, 0, 0, z, 0))] * dests,
        out_shape=[jax.ShapeDtypeStruct((modes, 2, 2, own_axial, radial), BF)] * dests,
        scratch_shapes=[
            pltpu.VMEM((3, block, angles, radial), BF),
            pltpu.VMEM((4 * dests, block, padded, radial), F32),
        ],
        compiler_params=pltpu.CompilerParams(vmem_limit_bytes=60 * 2**20),
        cost_estimate=pl.CostEstimate(
            flops=flops, bytes_accessed=8 * angles * own_axial * radial, transcendentals=0
        ),
        name="sums",
    )(velocity, adj_temp, radial_div, table, scale)


MESH = pl.DeviceIdType.MESH


def solve_kernel(
    chunks,
    lags,
    own_hbm,
    other_hbm,
    basis_hbm,
    diff_hbm,
    axial_ref,
    radial_ref,
    eig_ref,
    out_hbm,
    field_s,
    lines_s,
    cross_s,
    back_s,
    part_s,
    cross_o,
    back_o,
    own_s,
    basis_s,
    again_s,
    out_s,
    forward_s,
    diff_s,
    row_send,
    row_recv,
    ahead_send,
    ahead_recv,
    cross_send,
    cross_recv,
    back_send,
    back_recv,
    load_sem,
    out_sem,
):
    group, modes, big, width = lines_s.shape
    radial = field_s.shape[2]
    team = group // 2
    small = radial // team - big
    sizes = (big, small)
    starts = (0, team * big)
    count = modes // chunks
    half = width // 2
    own_axial = width // 4
    points = axial_ref.shape[0] // 2
    lag_axial, lag_add, lag_last = lags
    row_place = lax.axis_index("row")
    col_place = lax.axis_index("col")
    side = col_place // group
    place = col_place % group
    seat = place % team
    mine = (place // team + 1 - side) % 2
    across = {"row": 1 - row_place}

    def device(which, kind, number):
        return {"col": which * group + ((kind + 1 + which) % 2) * team + number}

    mirror = device(1 - side, mine, seat)

    def peer_seat(k):
        return (seat + k) % team

    def place_of(kind, k):
        return ((kind + 1 + side) % 2) * team + peer_seat(k)

    def each_peer(act):
        for kind in range(2):
            for k in range(team):
                if k == 0:
                    pl.when(mine != kind)(functools.partial(act, kind, k))
                else:
                    act(kind, k)

    def span(c):
        return pl.ds(c * count, count)

    def rows_of(kind, number):
        first = starts[kind] + number * sizes[kind]
        return pl.ds(pl.multiple_of(first, math.gcd(*sizes)), sizes[kind])

    def row_copy(c):
        return pltpu.make_async_remote_copy(
            src_ref=other_hbm.at[span(c)],
            dst_ref=field_s.at[span(c)],
            send_sem=row_send.at[c],
            recv_sem=row_recv.at[c],
            device_id=across,
            device_id_type=MESH,
        )

    def ahead_copy(c, kind, k):
        return pltpu.make_async_remote_copy(
            src_ref=field_s.at[span(c), rows_of(kind, peer_seat(k))],
            dst_ref=lines_s.at[place, span(c), pl.ds(0, sizes[kind])],
            send_sem=ahead_send.at[c % 2, kind, k],
            recv_sem=ahead_recv.at[c, mine, k],
            device_id=device(side, kind, peer_seat(k)),
            device_id_type=MESH,
        )

    def ahead_come(c, own_kind, kind, k):
        part = pl.ds(0, sizes[own_kind])
        return pltpu.make_async_remote_copy(
            src_ref=field_s.at[span(c), part],
            dst_ref=lines_s.at[place, span(c), part],
            send_sem=ahead_send.at[c % 2, kind, k],
            recv_sem=ahead_recv.at[c, kind, k],
            device_id=device(side, kind, peer_seat(k)),
            device_id_type=MESH,
        )

    def cross_copy(c, own_kind):
        part = pl.ds(0, sizes[own_kind])
        return pltpu.make_async_remote_copy(
            src_ref=cross_o.at[c % 2, :, :, part],
            dst_ref=cross_s.at[c, :, :, part],
            send_sem=cross_send.at[c % 2],
            recv_sem=cross_recv.at[c],
            device_id=mirror,
            device_id_type=MESH,
        )

    def back_copy(c, own_kind, kind, k):
        return pltpu.make_async_remote_copy(
            src_ref=back_o.at[c % 2, place_of(kind, k), :, pl.ds(0, sizes[own_kind])],
            dst_ref=back_s.at[span(c), rows_of(own_kind, seat)],
            send_sem=back_send.at[c % 2, kind, k],
            recv_sem=back_recv.at[c, own_kind, k],
            device_id=device(side, kind, peer_seat(k)),
            device_id_type=MESH,
        )

    def back_come(c, kind, k):
        return pltpu.make_async_remote_copy(
            src_ref=back_o.at[c % 2, place, :, pl.ds(0, sizes[kind])],
            dst_ref=back_s.at[span(c), rows_of(kind, seat)],
            send_sem=back_send.at[c % 2, kind, k],
            recv_sem=back_recv.at[c, kind, k],
            device_id=device(side, kind, peer_seat(k)),
            device_id_type=MESH,
        )

    def own_load(c):
        return pltpu.make_async_copy(own_hbm.at[span(c)], own_s.at[c % 2], load_sem.at[0, c % 2])

    def basis_load(c):
        return pltpu.make_async_copy(basis_hbm.at[span(c)], basis_s.at[c % 2], load_sem.at[1, c % 2])

    def again_load(c):
        return pltpu.make_async_copy(basis_hbm.at[span(c)], again_s.at[c % 2], load_sem.at[2, c % 2])

    def out_copy(c):
        return pltpu.make_async_copy(out_s.at[c % 2], out_hbm.at[span(c)], out_sem.at[c % 2])

    near = pl.multiple_of(side * points, points)
    diff_load = pltpu.make_async_copy(diff_hbm.at[:, pl.ds(near, points)], diff_s, load_sem.at[3, 0])
    diff_load.start()
    own_load(0).start()
    basis_load(0).start()
    again_load(0).start()
    barrier = pltpu.get_barrier_semaphore()

    def greet(target):
        pl.semaphore_signal(barrier, inc=1, device_id=target, device_id_type=MESH)

    greet(across)
    greet(mirror)
    each_peer(lambda kind, k: greet(device(side, kind, peer_seat(k))))
    pl.semaphore_wait(barrier, group + 1)

    def send_row(c, carry):
        row_copy(c).start()
        return carry

    lax.fori_loop(0, chunks, send_row, 0)
    diff_load.wait()
    turned = lax.dot_general(
        diff_s[...], axial_ref[...], (((0,), (0,)), ((), ())), preferred_element_type=F32
    ).astype(BF)
    for s in range(group):
        first = pl.multiple_of(near + s * own_axial, own_axial)
        forward_s[s * half : s * half + own_axial] = axial_ref[pl.ds(first, own_axial), :]
        forward_s[s * half + own_axial : (s + 1) * half] = turned[s * own_axial : (s + 1) * own_axial]

    def radial_part(c):
        own_load(c).wait()
        basis_load(c).wait()

        @pl.when(c + 1 < chunks)
        def _():
            own_load(c + 1).start()
            basis_load(c + 1).start()

        @pl.when(c >= 2)
        def _():
            each_peer(lambda kind, k: ahead_copy(c - 2, kind, k).wait_send())

        row_copy(c).wait_recv()
        for m in range(count):
            mode = c * count + m
            total = own_s[c % 2, m].astype(F32) + field_s[mode].astype(F32)
            hat = lax.dot_general(
                basis_s[c % 2, m],
                total.astype(BF),
                (((0,), (1,)), ((), ())),
                preferred_element_type=F32,
            )
            field_s[mode] = hat.astype(BF)
        each_peer(lambda kind, k: ahead_copy(c, kind, k).start())
        for kind in range(2):

            @pl.when(mine == kind)
            def _():
                part = field_s[span(c), rows_of(kind, seat), :]
                lines_s[place, span(c), : sizes[kind], :] = part

    def axial_part(own_kind, c):
        size = sizes[own_kind]
        rows = count * size
        each_peer(lambda kind, k: ahead_come(c, own_kind, kind, k).wait_recv())

        @pl.when(c >= 2)
        def _():
            cross_copy(c - 2, own_kind).wait_send()

        lines = jnp.concatenate(
            [
                jnp.concatenate(
                    [
                        lines_s[s, span(c), :size, p * half : (p + 1) * half].reshape(rows, half)
                        for s in range(group)
                    ],
                    axis=1,
                )
                for p in range(2)
            ],
            axis=0,
        )
        coefficients = jnp.dot(lines, forward_s[...], preferred_element_type=F32)
        first = starts[own_kind] + seat * size
        chosen = (
            lax.broadcasted_iota(jnp.int32, (size, radial), 1)
            == lax.broadcasted_iota(jnp.int32, (size, radial), 0) + first
        )
        eigen = jnp.concatenate(
            [
                jnp.sum(
                    jnp.where(chosen, radial_ref[pl.ds(c * count + m, 1), :], 0.0),
                    axis=1,
                    keepdims=True,
                )
                for m in range(count)
            ],
            axis=0,
        )
        eigen = eigen + eig_ref[...] + HEAT_OFFSET
        coefficients = jnp.concatenate(
            [(coefficients[p * rows : (p + 1) * rows] / eigen).astype(BF) for p in range(2)], axis=0
        )
        for far in (True, False):
            first = pl.multiple_of((1 - side if far else side) * points, points)
            returned = lax.dot_general(
                coefficients,
                axial_ref[pl.ds(first, points), :],
                (((1,), (1,)), ((), ())),
                preferred_element_type=F32,
            )
            for s in range(group):
                own = slice(s * own_axial, (s + 1) * own_axial)
                pair = jnp.concatenate([returned[:rows, own], returned[rows:, own]], axis=1)
                pair = pair.reshape(count, size, half)
                if far:
                    cross_o[c % 2, s, :, :size] = pair.astype(BF)
                else:
                    part_s[c % part_s.shape[0], s, :, :size] = pair
            if far:
                cross_copy(c, own_kind).start()

    def add_part(own_kind, c):
        size = sizes[own_kind]
        cross_copy(c, own_kind).wait_recv()

        @pl.when(c >= 2)
        def _():
            each_peer(lambda kind, k: back_copy(c - 2, own_kind, kind, k).wait_send())

        total = part_s[c % part_s.shape[0], :, :, :size] + cross_s[c, :, :, :size].astype(F32)
        back_o[c % 2, :, :, :size] = total.astype(BF)
        each_peer(lambda kind, k: back_copy(c, own_kind, kind, k).start())
        back_s[span(c), rows_of(own_kind, seat), :] = back_o[c % 2, place, :, :size]

    def last_part(c):
        again_load(c).wait()

        @pl.when(c + 1 < chunks)
        def _():
            again_load(c + 1).start()

        @pl.when(c >= 2)
        def _():
            out_copy(c - 2).wait()

        each_peer(lambda kind, k: back_come(c, kind, k).wait_recv())
        for m in range(count):
            out_s[c % 2, m] = lax.dot_general(
                back_s[c * count + m],
                again_s[c % 2, m],
                (((0,), (1,)), ((), ())),
                preferred_element_type=F32,
            ).reshape(out_s.shape[2:])
        out_copy(c).start()

    def step(s, carry):
        def live(lag):
            return (s >= lag) & (s < chunks + lag)

        pl.when(live(0))(functools.partial(radial_part, s))
        for kind in range(2):
            add = functools.partial(add_part, kind, s - lag_add)
            pl.when(live(lag_add) & (mine == kind))(add)
        for kind in range(2):
            solve_lines = functools.partial(axial_part, kind, s - lag_axial)
            pl.when(live(lag_axial) & (mine == kind))(solve_lines)
        pl.when(live(lag_last))(functools.partial(last_part, s - lag_last))
        return carry

    lax.fori_loop(0, chunks + lag_last, step, 0)

    def row_done(c, carry):
        row_copy(c).wait_send()
        return carry

    lax.fori_loop(0, chunks, row_done, 0)
    for c in range(chunks - 2, chunks):
        each_peer(lambda kind, k: ahead_copy(c, kind, k).wait_send())
        for own_kind in range(2):

            @pl.when(mine == own_kind)
            def _():
                each_peer(lambda kind, k: back_copy(c, own_kind, kind, k).wait_send())
                cross_copy(c, own_kind).wait_send()

        out_copy(c).wait()


def solve(own, other, basis, axial_diff, axial_basis, radial_eig, axial_eig, group, chunks, lags):
    modes, radial, _ = basis.shape
    width = own.shape[1]
    points = axial_basis.shape[0]
    team = group // 2
    big = radial // group * BIG_SHARE // 4
    count = modes // chunks
    half = width // 2
    own_axial = width // 4
    anywhere = pl.BlockSpec(memory_space=pl.ANY)
    vmem = pl.BlockSpec(memory_space=pltpu.VMEM)
    dma = pltpu.SemaphoreType.DMA
    return pl.pallas_call(
        functools.partial(solve_kernel, chunks, lags),
        in_specs=[anywhere] * 4 + [vmem] * 3,
        out_specs=anywhere,
        out_shape=jax.ShapeDtypeStruct((modes, 2, own_axial, radial), F32),
        scratch_shapes=[
            pltpu.VMEM((modes, width, radial), BF),
            pltpu.VMEM((group, modes, big, width), BF),
            pltpu.VMEM((chunks, group, count, big, half), BF),
            pltpu.VMEM((modes, radial, half), BF),
            pltpu.VMEM((lags[1] - lags[0], group, count, big, half), F32),
            pltpu.VMEM((2, group, count, big, half), BF),
            pltpu.VMEM((2, group, count, big, half), BF),
            pltpu.VMEM((2, count, width, radial), BF),
            pltpu.VMEM((2, count, radial, radial), BF),
            pltpu.VMEM((2, count, radial, radial), BF),
            pltpu.VMEM((2, count, 2, own_axial, radial), F32),
            pltpu.VMEM((points, points), BF),
            pltpu.VMEM((points, points // 2), BF),
            dma((chunks,)),
            dma((chunks,)),
            dma((2, 2, team)),
            dma((chunks, 2, team)),
            dma((2,)),
            dma((chunks,)),
            dma((2, 2, team)),
            dma((chunks, 2, team)),
            dma((4, 2)),
            dma((2,)),
        ],
        compiler_params=pltpu.CompilerParams(
            collective_id=0, has_side_effects=True, vmem_limit_bytes=67043328
        ),
        cost_estimate=pl.CostEstimate(
            flops=8 * modes * radial // group * points * points,
            bytes_accessed=6 * modes * radial * width,
            transcendentals=0,
        ),
        name="solve",
    )(own, other, basis, axial_diff, axial_basis, radial_eig, axial_eig[None])


CHUNK_MODES = 3
LAGS = (1, 2, 3)
BIG_SHARE = 6


def fused_body(
    velocity,
    adj_temp,
    radial_div,
    reciprocal_distance,
    radial_basis,
    radial_eig,
    axial_diff,
    axial_basis,
    axial_eig,
):
    row_total = lax.axis_size("row")
    group = lax.axis_size("col") // 2
    row_place = lax.axis_index("row")
    modes = radial_basis.shape[0]
    angles, own_axial, radial_points = adj_temp.shape
    circle = angles * row_total
    padded = round_up(modes, 8)
    firsts = [row_place * modes, (1 - row_place) * modes]
    tables = jnp.stack(
        [wave_rows(first, padded, row_place * angles, angles, circle) for first in firsts]
    )
    mode_values = jnp.stack(
        [(first + jnp.arange(padded, dtype=jnp.int32)).astype(F32) for first in firsts]
    )
    own, other = both_sums(
        velocity, adj_temp, radial_div, tables, mode_values, reciprocal_distance, modes
    )
    return solve(
        own.reshape(modes, 4 * own_axial, radial_points),
        other.reshape(modes, 4 * own_axial, radial_points),
        radial_basis,
        axial_diff,
        axial_basis,
        radial_eig,
        axial_eig,
        group,
        modes // CHUNK_MODES,
        LAGS,
    )


def solution(mesh):
    in_specs = (
        P(None, "row", "col", None),
        P("row", "col", None),
        P(),
        P(),
        P("row", None, None),
        P("row", None),
        P(),
        P(),
        P(),
    )
    out_specs = P("row", None, "col", None)
    if mesh.shape["row"] == 2 and mesh.shape["col"] == 16:
        return jax.shard_map(
            fused_body, mesh=mesh, in_specs=in_specs, out_specs=out_specs, check_vma=False
        )
    return jax.shard_map(body, mesh=mesh, in_specs=in_specs, out_specs=out_specs, check_vma=False)
```

```python
import functools
import math

import jax
import jax.numpy as jnp
from jax import lax
from jax.experimental import pallas as pl
from jax.experimental.pallas import tpu as pltpu
from jax.sharding import PartitionSpec as P


HEAT_OFFSET = 1.0
BF = jnp.bfloat16
F32 = jnp.float32


def wave_rows(first_mode, mode_count, first_angle, angle_count, circle):
    mode_ids = first_mode + jnp.arange(mode_count, dtype=jnp.int32)
    angle_ids = first_angle + jnp.arange(angle_count, dtype=jnp.int32)
    phase_index = mode_ids[:, None] * angle_ids[None, :] % circle
    angle_value = phase_index.astype(F32) * (2.0 * math.pi / circle)
    norm_factor = 1.0 / math.sqrt(circle)
    table = jnp.stack(
        [jnp.cos(angle_value) * norm_factor, -jnp.sin(angle_value) * norm_factor], axis=1
    )
    return table.astype(BF)


def chunk_count(modes):
    return max(c for c in range(1, 5) if modes % c == 0)


def round_up(value, unit):
    return -(-value // unit) * unit


def sums_kernel(modes, padded, vel_ref, adj_ref, div_ref, table_ref, scale_ref, *refs):
    *out_refs, field_s, sum_s = refs
    angles, block, radial = adj_ref.shape
    adj = adj_ref[...].astype(F32)
    for f in range(3):
        flux = (vel_ref[f].astype(F32) * adj).astype(BF)
        if f == 0:
            moved = lax.dot_general(
                flux.reshape(angles * block, radial),
                div_ref[...],
                (((1,), (1,)), ((), ())),
                preferred_element_type=F32,
            ).reshape(angles, block, radial)
            flux = (HEAT_OFFSET * adj + moved).astype(BF)
        field_s[f] = jnp.swapaxes(flux, 0, 1)

    def one(z, carry):
        heat, turn, flux = (
            jnp.dot(table_ref[...], field_s[f, z], preferred_element_type=F32) for f in range(3)
        )
        scale = scale_ref[...]
        sum_s[0, z] = heat[:padded] - scale * turn[padded:]
        sum_s[1, z] = flux[:padded]
        sum_s[2, z] = heat[padded:] + scale * turn[:padded]
        sum_s[3, z] = flux[padded:]
        return carry

    lax.fori_loop(0, block, one, 0)
    for k in range(4):
        turned = jnp.swapaxes(sum_s[k], 0, 1)
        step = modes // len(out_refs)
        for c, out_ref in enumerate(out_refs):
            out_ref[:, k // 2, k % 2] = turned[c * step : (c + 1) * step].astype(BF)


def azimuth_sums(velocity, adj_temp, radial_div, table, mode_values, reciprocal_distance, parts):
    modes = table.shape[0]
    angles, own_axial, radial = adj_temp.shape
    padded = round_up(modes, 8)
    block = 16 if own_axial % 16 == 0 else own_axial
    table = jnp.pad(jnp.moveaxis(table, 1, 0), ((0, 0), (0, padded - modes), (0, 0)))
    table = table.reshape(2 * padded, angles)
    scale = jnp.pad(
        mode_values[:, None] * reciprocal_distance[None], ((0, padded - modes), (0, 0))
    )
    flops = 2 * own_axial * radial * angles * (radial + 6 * padded)
    return pl.pallas_call(
        functools.partial(sums_kernel, modes, padded),
        grid=(own_axial // block,),
        in_specs=[
            pl.BlockSpec((3, angles, block, radial), lambda z: (0, 0, z, 0)),
            pl.BlockSpec((angles, block, radial), lambda z: (0, z, 0)),
            pl.BlockSpec((radial, radial), lambda z: (0, 0)),
            pl.BlockSpec((2 * padded, angles), lambda z: (0, 0)),
            pl.BlockSpec((padded, radial), lambda z: (0, 0)),
        ],
        out_specs=[
            pl.BlockSpec((modes // parts, 2, 2, block, radial), lambda z: (0, 0, 0, z, 0))
        ]
        * parts,
        out_shape=[jax.ShapeDtypeStruct((modes // parts, 2, 2, own_axial, radial), BF)] * parts,
        scratch_shapes=[
            pltpu.VMEM((3, block, angles, radial), BF),
            pltpu.VMEM((4, block, padded, radial), F32),
        ],
        compiler_params=pltpu.CompilerParams(vmem_limit_bytes=60 * 2**20),
        cost_estimate=pl.CostEstimate(
            flops=flops, bytes_accessed=8 * angles * own_axial * radial, transcendentals=0
        ),
        name="sums",
    )(velocity, adj_temp, radial_div, table, scale)


def radial_kernel(count, *refs):
    own_ref, others, basis_ref, out_ref = refs[0], refs[1:-2], refs[-2], refs[-1]
    radial = basis_ref.shape[1]
    for m in range(count):
        total = own_ref[m].astype(F32)
        for other in others:
            total = total + other[m].astype(F32)
        width = total.shape[0] * total.shape[1] * total.shape[2]
        hat = lax.dot_general(
            basis_ref[m],
            total.astype(BF).reshape(width, radial),
            (((0,), (1,)), ((), ())),
            preferred_element_type=F32,
        ).astype(BF)
        out_ref[:, m] = hat.reshape(out_ref.shape[0], out_ref.shape[2], width)


def radial_forward(own, others, basis, first, step, col_total):
    radial = basis.shape[1]
    width = 4 * own.shape[3]
    count = max(c for c in range(1, 8) if step % c == 0)
    skip = first // count
    field = (count, 2, 2, own.shape[3], radial)
    return pl.pallas_call(
        functools.partial(radial_kernel, count),
        grid=(step // count,),
        in_specs=[pl.BlockSpec(field, lambda m: (m, 0, 0, 0, 0)) for _ in (own, *others)]
        + [pl.BlockSpec((count, radial, radial), lambda m: (m + skip, 0, 0))],
        out_specs=pl.BlockSpec(
            (col_total, count, radial // col_total, width), lambda m: (0, m, 0, 0)
        ),
        out_shape=jax.ShapeDtypeStruct((col_total, step, radial // col_total, width), BF),
        compiler_params=pltpu.CompilerParams(vmem_limit_bytes=60 * 2**20),
        cost_estimate=pl.CostEstimate(
            flops=2 * step * radial * radial * width,
            bytes_accessed=2 * step * radial * (radial + 3 * width),
            transcendentals=0,
        ),
        name="radial",
    )(own, *others, basis)


def axial_kernel(lines_ref, forward_ref, basis_ref, radial_ref, axial_ref, out_ref):
    col_total, count, own_count, width = lines_ref.shape
    half = width // 2
    quarter = width // 4
    rows = count * own_count
    lines = jnp.concatenate(
        [
            jnp.concatenate(
                [
                    lines_ref[s, :, :, p * half : (p + 1) * half].reshape(rows, half)
                    for s in range(col_total)
                ],
                axis=1,
            )
            for p in range(2)
        ],
        axis=0,
    )
    coefficients = jnp.dot(lines, forward_ref[...], preferred_element_type=F32)
    eigen = radial_ref[...] + axial_ref[...] + HEAT_OFFSET
    coefficients = jnp.concatenate([coefficients[:rows] / eigen, coefficients[rows:] / eigen], axis=0)
    returned = lax.dot_general(
        coefficients.astype(BF),
        basis_ref[...],
        (((1,), (1,)), ((), ())),
        preferred_element_type=F32,
    )
    for s in range(col_total):
        own = slice(s * quarter, (s + 1) * quarter)
        pair = jnp.concatenate([returned[:rows, own], returned[rows:, own]], axis=1)
        out_ref[s] = pair.astype(BF).reshape(count, own_count, half)


def axial_solve(lines, forward, axial_basis, radial_values, axial_eig):
    col_total, step, own_count, width = lines.shape
    points = axial_basis.shape[0]
    count = max(c for c in range(1, 8) if step % c == 0)
    rows = step * own_count
    return pl.pallas_call(
        axial_kernel,
        grid=(step // count,),
        in_specs=[
            pl.BlockSpec((col_total, count, own_count, width), lambda m: (0, m, 0, 0)),
            pl.BlockSpec((2 * points, points), lambda m: (0, 0)),
            pl.BlockSpec((points, points), lambda m: (0, 0)),
            pl.BlockSpec((count * own_count, 1), lambda m: (m, 0)),
            pl.BlockSpec((1, points), lambda m: (0, 0)),
        ],
        out_specs=pl.BlockSpec((col_total, count, own_count, width // 2), lambda m: (0, m, 0, 0)),
        out_shape=jax.ShapeDtypeStruct((col_total, step, own_count, width // 2), BF),
        compiler_params=pltpu.CompilerParams(vmem_limit_bytes=60 * 2**20),
        cost_estimate=pl.CostEstimate(
            flops=12 * rows * points * points,
            bytes_accessed=6 * points * points + 6 * rows * points,
            transcendentals=0,
        ),
        name="axial",
    )(lines, forward, axial_basis, radial_values.reshape(rows, 1), axial_eig.reshape(1, points))


def last_kernel(count, returned_ref, basis_ref, *refs):
    out_ref = refs[-1]
    for m in range(count):
        lines = returned_ref[:, m]
        lines = lines.reshape(lines.shape[0] * lines.shape[1], lines.shape[2])
        out_ref[m] = lax.dot_general(
            lines, basis_ref[m], (((0,), (1,)), ((), ())), preferred_element_type=F32
        ).reshape(out_ref.shape[1:])


def radial_back(returned, basis, before, first):
    col_total, step, own_count, width = returned.shape
    modes, radial, _ = basis.shape
    count = max(c for c in range(1, 8) if step % c == 0)
    skip = first // count
    return pl.pallas_call(
        functools.partial(last_kernel, count),
        grid=(step // count,),
        in_specs=[
            pl.BlockSpec((col_total, count, own_count, width), lambda m: (0, m, 0, 0)),
            pl.BlockSpec((count, radial, radial), lambda m: (m + skip, 0, 0)),
        ]
        + [pl.BlockSpec(memory_space=pl.ANY) for _ in before],
        out_specs=pl.BlockSpec((count, 2, width // 2, radial), lambda m: (m + skip, 0, 0, 0)),
        out_shape=jax.ShapeDtypeStruct((modes, 2, width // 2, radial), F32),
        input_output_aliases={2: 0} if before else {},
        compiler_params=pltpu.CompilerParams(vmem_limit_bytes=60 * 2**20),
        cost_estimate=pl.CostEstimate(
            flops=2 * step * radial * radial * width,
            bytes_accessed=2 * step * radial * (radial + 3 * width),
            transcendentals=0,
        ),
        name="last",
    )(returned, basis, *before)


def body(
    velocity,
    adj_temp,
    radial_div,
    reciprocal_distance,
    radial_basis,
    radial_eig,
    axial_diff,
    axial_basis,
    axial_eig,
):
    row_total = lax.axis_size("row")
    col_total = lax.axis_size("col")
    row_place = lax.axis_index("row")
    col_place = lax.axis_index("col")
    modes = radial_basis.shape[0]
    angles, own_axial, radial_points = adj_temp.shape
    axial_points = axial_basis.shape[0]
    own_count = radial_points // col_total
    circle = angles * row_total
    parts = chunk_count(modes)
    step = modes // parts

    def partial_sums(place):
        table = wave_rows(place * modes, modes, row_place * angles, angles, circle)
        mode_values = (place * modes + jnp.arange(modes, dtype=jnp.int32)).astype(F32)
        return azimuth_sums(
            velocity, adj_temp, radial_div, table, mode_values, reciprocal_distance, parts
        )

    arrived = [[] for _ in range(parts)]
    for shift in range(1, row_total):
        sums = partial_sums((row_place + shift) % row_total)
        pairs = [(a, (a + shift) % row_total) for a in range(row_total)]
        for c in range(parts):
            arrived[c].append(lax.ppermute(sums[c], "row", pairs))
    own = partial_sums(row_place)

    returning = jnp.einsum("zj,zk->jk", axial_diff, axial_basis, preferred_element_type=F32)
    forward = jnp.stack(
        [
            axial_basis.reshape(col_total, own_axial, axial_points),
            returning.astype(BF).reshape(col_total, own_axial, axial_points),
        ],
        axis=1,
    )
    axial_blocks = axial_basis.reshape(col_total, own_axial, axial_points)
    radial_values = lax.dynamic_slice_in_dim(radial_eig, col_place * own_count, own_count, 1)

    fits = own_axial % 64 == 0 and own_count % 16 == 0
    outs = []
    new_temp = ()
    for c in range(parts):
        part = slice(c * step, (c + 1) * step)
        hat = radial_forward(own[c], arrived[c], radial_basis, c * step, step, col_total)
        lines = lax.all_to_all(hat, "col", split_axis=0, concat_axis=0, tiled=True)
        if fits:
            returned = axial_solve(
                lines,
                forward.reshape(2 * axial_points, axial_points),
                axial_basis,
                radial_values[part],
                axial_eig,
            )
        else:
            lines = lines.reshape(col_total, step, own_count, 2, 2, own_axial)
            coefficients = jnp.einsum(
                "smxpfy,sfyk->pmxk", lines, forward, preferred_element_type=F32
            )
            coefficients = coefficients / (
                radial_values[part][None, :, :, None] + axial_eig + HEAT_OFFSET
            )
            returned = jnp.einsum(
                "pmxk,syk->smxpy", coefficients.astype(BF), axial_blocks, preferred_element_type=F32
            ).astype(BF)
            returned = returned.reshape(col_total, step, own_count, 2 * own_axial)
        returned = lax.all_to_all(returned, "col", split_axis=0, concat_axis=0, tiled=True)
        if fits:
            new_temp = (radial_back(returned, radial_basis, new_temp, c * step),)
            continue
        returned = jnp.moveaxis(returned, 0, 1).reshape(step, radial_points, 2 * own_axial)
        outs.append(
            jnp.einsum("miw,mri->mwr", returned, radial_basis[part], preferred_element_type=F32).reshape(
                step, 2, own_axial, radial_points
            )
        )
    return new_temp[0] if fits else jnp.concatenate(outs, axis=0)


def both_sums_kernel(modes, padded, vel_ref, adj_ref, div_ref, table_ref, scale_ref, *refs):
    *out_refs, field_s, sum_s = refs
    angles, block, radial = adj_ref.shape
    for f in range(3):
        flux = vel_ref[f] * adj_ref[...]
        if f == 0:
            moved = lax.dot_general(
                flux.reshape(angles * block, radial),
                div_ref[...],
                (((1,), (1,)), ((), ())),
                preferred_element_type=F32,
            ).reshape(angles, block, radial)
            flux = (HEAT_OFFSET * adj_ref[...].astype(F32) + moved).astype(BF)
        field_s[f] = jnp.swapaxes(flux, 0, 1)

    def one(z, carry):
        heat, turn, flux = (
            jnp.dot(table_ref[...], field_s[f, z], preferred_element_type=F32) for f in range(3)
        )
        for d in range(len(out_refs)):
            re = slice(2 * d * padded, (2 * d + 1) * padded)
            im = slice((2 * d + 1) * padded, (2 * d + 2) * padded)
            scale = scale_ref[d]
            sum_s[4 * d, z] = (heat[re] - scale * turn[im]).astype(BF)
            sum_s[4 * d + 1, z] = (flux[re]).astype(BF)
            sum_s[4 * d + 2, z] = (heat[im] + scale * turn[re]).astype(BF)
            sum_s[4 * d + 3, z] = (flux[im]).astype(BF)
        return carry

    lax.fori_loop(0, block, one, 0)
    for d, out_ref in enumerate(out_refs):
        for k in range(4):
            turned = jnp.swapaxes(sum_s[4 * d + k], 0, 1)
            out_ref[:, k // 2, k % 2] = turned[:modes]


def both_sums(
    velocity, adj_temp, radial_div, tables, mode_values, reciprocal_distance, modes
):
    dests, padded = mode_values.shape
    angles, own_axial, radial = adj_temp.shape
    block = 16 if own_axial % 16 == 0 else own_axial
    table = jnp.moveaxis(tables, 2, 1).reshape(dests * 2 * padded, angles)
    scale = mode_values[:, :, None] * reciprocal_distance[None, None]
    flops = 2 * own_axial * radial * angles * (radial + 6 * padded * dests)
    return pl.pallas_call(
        functools.partial(both_sums_kernel, modes, padded),
        grid=(own_axial // block,),
        in_specs=[
            pl.BlockSpec((3, angles, block, radial), lambda z: (0, 0, z, 0)),
            pl.BlockSpec((angles, block, radial), lambda z: (0, z, 0)),
            pl.BlockSpec((radial, radial), lambda z: (0, 0)),
            pl.BlockSpec((dests * 2 * padded, angles), lambda z: (0, 0)),
            pl.BlockSpec((dests, padded, radial), lambda z: (0, 0, 0)),
        ],
        out_specs=[pl.BlockSpec((modes, 2, 2, block, radial), lambda z: (0, 0, 0, z, 0))] * dests,
        out_shape=[jax.ShapeDtypeStruct((modes, 2, 2, own_axial, radial), BF)] * dests,
        scratch_shapes=[
            pltpu.VMEM((3, block, angles, radial), BF),
            pltpu.VMEM((4 * dests, block, padded, radial), BF),
        ],
        compiler_params=pltpu.CompilerParams(vmem_limit_bytes=60 * 2**20),
        cost_estimate=pl.CostEstimate(
            flops=flops, bytes_accessed=8 * angles * own_axial * radial, transcendentals=0
        ),
        name="sums",
    )(velocity, adj_temp, radial_div, table, scale)


MESH = pl.DeviceIdType.MESH


def solve_kernel(
    chunks,
    lags,
    own_hbm,
    other_hbm,
    basis_hbm,
    diff_hbm,
    axial_ref,
    radial_ref,
    eig_ref,
    out_hbm,
    field_s,
    lines_s,
    cross_s,
    back_s,
    part_s,
    cross_o,
    back_o,
    own_s,
    basis_s,
    again_s,
    out_s,
    forward_s,
    diff_s,
    row_send,
    row_recv,
    ahead_send,
    ahead_recv,
    cross_send,
    cross_recv,
    back_send,
    back_recv,
    load_sem,
    out_sem,
):
    group, modes, big, width = lines_s.shape
    radial = field_s.shape[2]
    team = group // 2
    small = radial // team - big
    sizes = (big, small)
    starts = (0, team * big)
    count = modes // chunks
    half = width // 2
    own_axial = width // 4
    points = axial_ref.shape[0] // 2
    lag_axial, lag_add, lag_last = lags
    row_place = lax.axis_index("row")
    col_place = lax.axis_index("col")
    side = col_place // group
    place = col_place % group
    seat = place % team
    mine = (place // team + 1 - side) % 2
    across = {"row": 1 - row_place}

    def device(which, kind, number):
        return {"col": which * group + ((kind + 1 + which) % 2) * team + number}

    mirror = device(1 - side, mine, seat)

    def peer_seat(k):
        return (seat + k) % team

    def place_of(kind, k):
        return ((kind + 1 + side) % 2) * team + peer_seat(k)

    solvers = [kind for kind in range(2) if sizes[kind]]

    def each_peer(act, kinds=(0, 1)):
        for kind in kinds:
            for k in range(team):
                if k == 0:
                    pl.when(mine != kind)(functools.partial(act, kind, k))
                else:
                    act(kind, k)

    def span(c):
        return pl.ds(c * count, count)

    def rows_of(kind, number):
        first = starts[kind] + number * sizes[kind]
        return pl.ds(pl.multiple_of(first, math.gcd(*sizes)), sizes[kind])

    def row_copy(c):
        return pltpu.make_async_remote_copy(
            src_ref=other_hbm.at[span(c)],
            dst_ref=field_s.at[span(c)],
            send_sem=row_send.at[c],
            recv_sem=row_recv.at[c],
            device_id=across,
            device_id_type=MESH,
        )

    def ahead_copy(c, kind, k):
        return pltpu.make_async_remote_copy(
            src_ref=field_s.at[span(c), rows_of(kind, peer_seat(k))],
            dst_ref=lines_s.at[place, span(c), pl.ds(0, sizes[kind])],
            send_sem=ahead_send.at[c % 2, kind, k],
            recv_sem=ahead_recv.at[c, mine, k],
            device_id=device(side, kind, peer_seat(k)),
            device_id_type=MESH,
        )

    def ahead_come(c, own_kind, kind, k):
        part = pl.ds(0, sizes[own_kind])
        return pltpu.make_async_remote_copy(
            src_ref=field_s.at[span(c), part],
            dst_ref=lines_s.at[place, span(c), part],
            send_sem=ahead_send.at[c % 2, kind, k],
            recv_sem=ahead_recv.at[c, kind, k],
            device_id=device(side, kind, peer_seat(k)),
            device_id_type=MESH,
        )

    def cross_copy(c, own_kind):
        part = pl.ds(0, sizes[own_kind])
        return pltpu.make_async_remote_copy(
            src_ref=cross_o.at[c % 2, :, :, part],
            dst_ref=cross_s.at[c, :, :, part],
            send_sem=cross_send.at[c % 2],
            recv_sem=cross_recv.at[c],
            device_id=mirror,
            device_id_type=MESH,
        )

    def back_copy(c, own_kind, kind, k):
        return pltpu.make_async_remote_copy(
            src_ref=back_o.at[c % 2, place_of(kind, k), :, pl.ds(0, sizes[own_kind])],
            dst_ref=back_s.at[span(c), rows_of(own_kind, seat)],
            send_sem=back_send.at[c % 2, kind, k],
            recv_sem=back_recv.at[c, own_kind, k],
            device_id=device(side, kind, peer_seat(k)),
            device_id_type=MESH,
        )

    def back_come(c, kind, k):
        return pltpu.make_async_remote_copy(
            src_ref=back_o.at[c % 2, place, :, pl.ds(0, sizes[kind])],
            dst_ref=back_s.at[span(c), rows_of(kind, seat)],
            send_sem=back_send.at[c % 2, kind, k],
            recv_sem=back_recv.at[c, kind, k],
            device_id=device(side, kind, peer_seat(k)),
            device_id_type=MESH,
        )

    def own_load(c):
        return pltpu.make_async_copy(own_hbm.at[span(c)], own_s.at[c % 2], load_sem.at[0, c % 2])

    def basis_load(c):
        return pltpu.make_async_copy(basis_hbm.at[span(c)], basis_s.at[c % 2], load_sem.at[1, c % 2])

    def again_load(c):
        return pltpu.make_async_copy(basis_hbm.at[span(c)], again_s.at[c % 2], load_sem.at[2, c % 2])

    def out_copy(c):
        return pltpu.make_async_copy(out_s.at[c % 2], out_hbm.at[span(c)], out_sem.at[c % 2])

    near = pl.multiple_of(side * points, points)
    diff_load = pltpu.make_async_copy(diff_hbm.at[:, pl.ds(near, points)], diff_s, load_sem.at[3, 0])
    diff_load.start()
    own_load(0).start()
    basis_load(0).start()
    again_load(0).start()
    barrier = pltpu.get_barrier_semaphore()

    def greet(target):
        pl.semaphore_signal(barrier, inc=1, device_id=target, device_id_type=MESH)

    greet(across)
    greet(mirror)
    each_peer(lambda kind, k: greet(device(side, kind, peer_seat(k))))
    pl.semaphore_wait(barrier, group + 1)

    def send_row(c, carry):
        row_copy(c).start()
        return carry

    lax.fori_loop(0, chunks, send_row, 0)
    diff_load.wait()
    turned = lax.dot_general(
        diff_s[...], axial_ref[...], (((0,), (0,)), ((), ())), preferred_element_type=F32
    ).astype(BF)
    for s in range(group):
        first = pl.multiple_of(near + s * own_axial, own_axial)
        forward_s[s * half : s * half + own_axial] = axial_ref[pl.ds(first, own_axial), :]
        forward_s[s * half + own_axial : (s + 1) * half] = turned[s * own_axial : (s + 1) * own_axial]

    def radial_part(c):
        own_load(c).wait()
        basis_load(c).wait()

        @pl.when(c + 1 < chunks)
        def _():
            own_load(c + 1).start()
            basis_load(c + 1).start()

        @pl.when(c >= 2)
        def _():
            each_peer(lambda kind, k: ahead_copy(c - 2, kind, k).wait_send(), solvers)

        row_copy(c).wait_recv()
        for m in range(count):
            mode = c * count + m
            total = own_s[c % 2, m].astype(F32) + field_s[mode].astype(F32)
            hat = lax.dot_general(
                basis_s[c % 2, m],
                total.astype(BF),
                (((0,), (1,)), ((), ())),
                preferred_element_type=F32,
            )
            field_s[mode] = hat.astype(BF)
        each_peer(lambda kind, k: ahead_copy(c, kind, k).start(), solvers)
        for kind in solvers:

            @pl.when(mine == kind)
            def _():
                part = field_s[span(c), rows_of(kind, seat), :]
                lines_s[place, span(c), : sizes[kind], :] = part

    def axial_part(own_kind, c):
        size = sizes[own_kind]
        rows = count * size
        each_peer(lambda kind, k: ahead_come(c, own_kind, kind, k).wait_recv())

        @pl.when(c >= 2)
        def _():
            cross_copy(c - 2, own_kind).wait_send()

        lines = jnp.concatenate(
            [
                jnp.concatenate(
                    [
                        lines_s[s, span(c), :size, p * half : (p + 1) * half].reshape(rows, half)
                        for s in range(group)
                    ],
                    axis=1,
                )
                for p in range(2)
            ],
            axis=0,
        )
        coefficients = jnp.dot(lines, forward_s[...], preferred_element_type=F32)
        first = starts[own_kind] + seat * size
        chosen = (
            lax.broadcasted_iota(jnp.int32, (size, radial), 1)
            == lax.broadcasted_iota(jnp.int32, (size, radial), 0) + first
        )
        eigen = jnp.concatenate(
            [
                jnp.sum(
                    jnp.where(chosen, radial_ref[pl.ds(c * count + m, 1), :], 0.0),
                    axis=1,
                    keepdims=True,
                )
                for m in range(count)
            ],
            axis=0,
        )
        eigen = eigen + eig_ref[...] + HEAT_OFFSET
        coefficients = jnp.concatenate(
            [(coefficients[p * rows : (p + 1) * rows] / eigen).astype(BF) for p in range(2)], axis=0
        )
        for far in (True, False):
            first = pl.multiple_of((1 - side if far else side) * points, points)
            returned = lax.dot_general(
                coefficients,
                axial_ref[pl.ds(first, points), :],
                (((1,), (1,)), ((), ())),
                preferred_element_type=F32,
            )
            for s in range(group):
                own = slice(s * own_axial, (s + 1) * own_axial)
                pair = jnp.concatenate([returned[:rows, own], returned[rows:, own]], axis=1)
                pair = pair.reshape(count, size, half)
                if far:
                    cross_o[c % 2, s, :, :size] = pair.astype(BF)
                else:
                    part_s[c % part_s.shape[0], s, :, :size] = pair
            if far:
                cross_copy(c, own_kind).start()

    def add_part(own_kind, c):
        size = sizes[own_kind]
        cross_copy(c, own_kind).wait_recv()

        @pl.when(c >= 2)
        def _():
            each_peer(lambda kind, k: back_copy(c - 2, own_kind, kind, k).wait_send())

        total = part_s[c % part_s.shape[0], :, :, :size] + cross_s[c, :, :, :size].astype(F32)
        back_o[c % 2, :, :, :size] = total.astype(BF)
        each_peer(lambda kind, k: back_copy(c, own_kind, kind, k).start())
        back_s[span(c), rows_of(own_kind, seat), :] = back_o[c % 2, place, :, :size]

    def last_part(c):
        again_load(c).wait()

        @pl.when(c + 1 < chunks)
        def _():
            again_load(c + 1).start()

        @pl.when(c >= 2)
        def _():
            out_copy(c - 2).wait()

        each_peer(lambda kind, k: back_come(c, kind, k).wait_recv(), solvers)
        for m in range(count):
            out_s[c % 2, m] = lax.dot_general(
                back_s[c * count + m],
                again_s[c % 2, m],
                (((0,), (1,)), ((), ())),
                preferred_element_type=F32,
            ).astype(BF).reshape(out_s.shape[2:])
        out_copy(c).start()

    def step(s, carry):
        def live(lag):
            return (s >= lag) & (s < chunks + lag)

        pl.when(live(0))(functools.partial(radial_part, s))
        for kind in solvers:
            add = functools.partial(add_part, kind, s - lag_add)
            pl.when(live(lag_add) & (mine == kind))(add)
        for kind in solvers:
            solve_lines = functools.partial(axial_part, kind, s - lag_axial)
            pl.when(live(lag_axial) & (mine == kind))(solve_lines)
        pl.when(live(lag_last))(functools.partial(last_part, s - lag_last))
        return carry

    lax.fori_loop(0, chunks + lag_last, step, 0)

    def row_done(c, carry):
        row_copy(c).wait_send()
        return carry

    lax.fori_loop(0, chunks, row_done, 0)
    for c in range(chunks - 2, chunks):
        each_peer(lambda kind, k: ahead_copy(c, kind, k).wait_send(), solvers)
        for own_kind in solvers:

            @pl.when(mine == own_kind)
            def _():
                each_peer(lambda kind, k: back_copy(c, own_kind, kind, k).wait_send())
                cross_copy(c, own_kind).wait_send()

        out_copy(c).wait()


def solve(own, other, basis, axial_diff, axial_basis, radial_eig, axial_eig, group, chunks, lags):
    modes, radial, _ = basis.shape
    width = own.shape[1]
    points = axial_basis.shape[0]
    team = group // 2
    big = radial // group * BIG_SHARE // 4
    count = modes // chunks
    half = width // 2
    own_axial = width // 4
    anywhere = pl.BlockSpec(memory_space=pl.ANY)
    vmem = pl.BlockSpec(memory_space=pltpu.VMEM)
    dma = pltpu.SemaphoreType.DMA
    return pl.pallas_call(
        functools.partial(solve_kernel, chunks, lags),
        in_specs=[anywhere] * 4 + [vmem] * 3,
        out_specs=anywhere,
        out_shape=jax.ShapeDtypeStruct((modes, 2, own_axial, radial), BF),
        scratch_shapes=[
            pltpu.VMEM((modes, width, radial), BF),
            pltpu.VMEM((group, modes, big, width), BF),
            pltpu.VMEM((chunks, group, count, big, half), BF),
            pltpu.VMEM((modes, radial, half), BF),
            pltpu.VMEM((lags[1] - lags[0], group, count, big, half), F32),
            pltpu.VMEM((2, group, count, big, half), BF),
            pltpu.VMEM((2, group, count, big, half), BF),
            pltpu.VMEM((2, count, width, radial), BF),
            pltpu.VMEM((2, count, radial, radial), BF),
            pltpu.VMEM((2, count, radial, radial), BF),
            pltpu.VMEM((2, count, 2, own_axial, radial), BF),
            pltpu.VMEM((points, points), BF),
            pltpu.VMEM((points, points // 2), BF),
            dma((chunks,)),
            dma((chunks,)),
            dma((2, 2, team)),
            dma((chunks, 2, team)),
            dma((2,)),
            dma((chunks,)),
            dma((2, 2, team)),
            dma((chunks, 2, team)),
            dma((4, 2)),
            dma((2,)),
        ],
        compiler_params=pltpu.CompilerParams(
            collective_id=0, has_side_effects=True, vmem_limit_bytes=67043328
        ),
        cost_estimate=pl.CostEstimate(
            flops=8 * modes * radial // group * points * points,
            bytes_accessed=6 * modes * radial * width,
            transcendentals=0,
        ),
        name="solve",
    )(own, other, basis, axial_diff, axial_basis, radial_eig, axial_eig[None])


CHUNK_MODES = 2
LAGS = (1, 3, 4)
BIG_SHARE = 6


def fused_body(
    velocity,
    adj_temp,
    radial_div,
    reciprocal_distance,
    radial_basis,
    radial_eig,
    axial_diff,
    axial_basis,
    axial_eig,
):
    row_total = lax.axis_size("row")
    group = lax.axis_size("col") // 2
    row_place = lax.axis_index("row")
    modes = radial_basis.shape[0]
    angles, own_axial, radial_points = adj_temp.shape
    circle = angles * row_total
    padded = round_up(modes, 8)
    firsts = [row_place * modes, (1 - row_place) * modes]
    tables = jnp.stack(
        [wave_rows(first, padded, row_place * angles, angles, circle) for first in firsts]
    )
    mode_values = jnp.stack(
        [(first + jnp.arange(padded, dtype=jnp.int32)).astype(F32) for first in firsts]
    )
    own, other = both_sums(
        velocity, adj_temp, radial_div, tables, mode_values, reciprocal_distance, modes
    )
    return solve(
        own.reshape(modes, 4 * own_axial, radial_points),
        other.reshape(modes, 4 * own_axial, radial_points),
        radial_basis,
        axial_diff,
        axial_basis,
        radial_eig,
        axial_eig,
        group,
        modes // CHUNK_MODES,
        LAGS,
    ).astype(F32)


def solution(mesh):
    in_specs = (
        P(None, "row", "col", None),
        P("row", "col", None),
        P(),
        P(),
        P("row", None, None),
        P("row", None),
        P(),
        P(),
        P(),
    )
    out_specs = P("row", None, "col", None)
    if mesh.shape["row"] == 2 and mesh.shape["col"] == 16:
        return jax.shard_map(
            fused_body, mesh=mesh, in_specs=in_specs, out_specs=out_specs, check_vma=False
        )
    return jax.shard_map(body, mesh=mesh, in_specs=in_specs, out_specs=out_specs, check_vma=False)
```
